512 devices in a mesh: section: 4 (over x), row: 8 (over y, core), col: 16 (over z).
Axes of the slice: x: 4, y: 4, z: 16, core: 2. Of those that a mesh axis runs over, the one named last changes fastest.
Arguments:
- latent: bfloat16 [2, 128, 256, 128], P(None, 'row', 'col'), may hold values from -6 to 6
- hidden_old: bfloat16 [4, 2, 128, 256, 128], P('section', None, 'row', 'col'), may hold values from -1 to 1
- cell_old: float32 [4, 2, 128, 256, 128], P('section', None, 'row', 'col'), may hold values from -6 to 6
- weights: bfloat16 [4, 9, 256, 512], P('section'), may hold values from -0.125 to 0.125
- bias: float32 [4, 512], P('section'), may hold values from -3 to 3
Outputs:
- hidden_new: bfloat16 [4, 2, 128, 256, 128], P('section', None, 'row', 'col')
- cell_new: float32 [4, 2, 128, 256, 128], P('section', None, 'row', 'col')
The draws below stay inside these ranges and needn't reach their ends.
All inputs are finite; a program needn't handle non-finite values.
Results may differ from the reference program's by a relative error of at most 0.0016.
Values may be sent and summed in bfloat16 or wider, within the bound.
No kernel may reach another device: no remote copies, remote signals or barrier semaphores. Data moves between devices by JAX's collectives and lax.ppermute only.
A program may use at most 64 MiB of HBM per device.

```python
import jax
import jax.numpy as jnp

HIDDEN_SIZE = 128
GATES = 512
LAYERS = 4
BATCH = 2
GRID_H = 128
GRID_W = 256


def block_scale(own_key, dims, pieces, least, high):
    def one(position, blocks):
        heights = jax.random.uniform(jax.random.fold_in(jax.random.fold_in(own_key, 6), position), (blocks,), jnp.float32, least / len(pieces), high / len(pieces))
        return jnp.repeat(jnp.exp(heights), dims[position] // blocks).reshape((-1,) + (1,) * (len(dims) - position - 1))

    gain = one(*pieces[0])
    for cut in pieces[1:]:
        gain = gain * one(*cut)
    return gain


def bell_draw(rng, extent, scale, most, cuts=(), kind=jnp.bfloat16):
    entries = jax.random.normal(rng, extent, jnp.float32) * scale
    if len(cuts) > 0:
        entries = block_scale(rng, extent, cuts, -0.22, 0.18) * entries
    return jnp.clip(entries, min=-most, max=most).astype(kind)


def setup_inputs(seed: int = 0) -> dict:
    arg_keys = jax.random.split(jax.random.key(seed), 6)
    latent = bell_draw(arg_keys[0], (BATCH, GRID_H, GRID_W, HIDDEN_SIZE), 1.0, 6.0, ((1, 8), (2, 16)))
    hidden_old = jnp.clip(jax.random.uniform(arg_keys[1], (LAYERS, BATCH, GRID_H, GRID_W, HIDDEN_SIZE), jnp.float32, -1.0, 1.0) * block_scale(arg_keys[1], (LAYERS, BATCH, GRID_H, GRID_W, HIDDEN_SIZE), ((0, 4), (2, 8), (3, 16)), -0.4, 0.0), -1.0, 1.0).astype(jnp.bfloat16)
    cell_old = bell_draw(arg_keys[2], (LAYERS, BATCH, GRID_H, GRID_W, HIDDEN_SIZE), 1.0, 6.0, ((0, 4), (2, 8), (3, 16)), jnp.float32)
    weights = bell_draw(arg_keys[3], (LAYERS, 9, 2 * HIDDEN_SIZE, GATES), (18 * HIDDEN_SIZE) ** -0.5, 0.125, ((0, 4),))
    bias = bell_draw(arg_keys[4], (LAYERS, GATES), 0.5, 3.0, ((0, 4),), jnp.float32)
    return {"latent": latent, "hidden_old": hidden_old, "cell_old": cell_old, "weights": weights, "bias": bias}


def conv_layer(layer_in, hidden_prev, cell_prev, kernel, offset):
    stacked = jnp.concatenate([layer_in, hidden_prev], axis=-1)
    padded = jnp.pad(stacked, ((0, 0), (1, 1), (1, 1), (0, 0)))
    batch, height, width, chans = stacked.shape
    gates = jnp.zeros((batch * height * width, kernel.shape[-1]), jnp.float32)
    for tap in range(9):
        dy = tap // 3
        dx = tap % 3
        window = padded[:, dy:dy + height, dx:dx + width, :].reshape(-1, chans)
        gates = gates + jnp.dot(window, kernel[tap], preferred_element_type=jnp.float32)
    gates = (gates + offset[None, :]).reshape(batch, height, width, -1)
    quarter = gates.shape[-1] // 4
    gate_i = jax.nn.sigmoid(gates[..., :quarter])
    gate_f = jax.nn.sigmoid(gates[..., quarter:2 * quarter])
    gate_g = jnp.tanh(gates[..., 2 * quarter:3 * quarter])
    gate_o = jax.nn.sigmoid(gates[..., 3 * quarter:])
    cell = gate_f * cell_prev + gate_i * gate_g
    hidden = (gate_o * jnp.tanh(cell)).astype(jnp.bfloat16)
    return hidden, cell


def reference(latent, hidden_old, cell_old, weights, bias):
    layer_in = latent
    hiddens = []
    cells = []
    for layer in range(LAYERS):
        hidden, cell = conv_layer(layer_in, hidden_old[layer], cell_old[layer], weights[layer], bias[layer])
        hiddens.append(hidden)
        cells.append(cell)
        layer_in = hidden
    return jnp.stack(hiddens), jnp.stack(cells)
```

```python
import functools

import jax
import jax.numpy as jnp
from jax import lax
from jax.experimental import pallas as pl
from jax.experimental.pallas import tpu as pltpu
from jax.sharding import PartitionSpec as P

F32 = jnp.float32
BF16 = jnp.bfloat16


def sigmoid(x):
    return 0.5 * jnp.tanh(0.5 * x) + 0.5


def rolled(x, by):
    rows = x.shape[0]
    by = by % rows
    return x if by == 0 else pltpu.roll(x, rows - by, 0)


def layer_kernel(tick, batch, stride, tile, blocks, first, sec_ref, x_ref, hid_ref, cell_ref, w_ref, b_ref, m_ref, *rest):
    if first:
        hout_ref, cout_ref, send_ref, cols, htile, ctile, sems = rest
    else:
        _, _, hout_ref, cout_ref, send_ref, cols, htile, ctile, sems = rest
    edge = 3 - tick
    count = tile + 2 * edge
    rows = count * stride
    chans = 128

    @pl.when(sec_ref[0] == tick)
    def _():
        layer_in = (x_ref[batch] if tick == 0 else x_ref[...]).astype(F32)
        hidden = hid_ref[batch].astype(F32)
        for dx in range(3):
            xs = rolled(layer_in, dx)
            hs = rolled(hidden, tick + dx)
            for dy in range(3):
                at = (3 * dy + dx) * 2 * chans
                cols[:, at : at + chans] = xs[dy * stride : dy * stride + rows].astype(BF16)
                cols[:, at + chans : at + 2 * chans] = hs[
                    (tick + dy) * stride : (tick + dy) * stride + rows
                ].astype(BF16)
        cell_prev = rolled(cell_ref[batch], tick + 1)[(tick + 1) * stride : (tick + 1) * stride + rows]
        size = rows // blocks
        hs, cs = [], []
        for k in range(blocks):
            part = slice(k * size, (k + 1) * size)
            gates = jnp.dot(cols[part], w_ref[...], preferred_element_type=F32) + b_ref[...]
            cell = sigmoid(gates[:, chans : 2 * chans]) * cell_prev[part] + sigmoid(gates[:, :chans]) * jnp.tanh(
                gates[:, 2 * chans : 3 * chans]
            )
            hid = sigmoid(gates[:, 3 * chans :]) * jnp.tanh(cell)
            hs.append(hid * m_ref[part, :])
            cs.append(cell)
        hid = jnp.concatenate(hs, axis=0)
        cell = jnp.concatenate(cs, axis=0)
        send_ref[...] = hid.astype(BF16)
        mid = lambda v: rolled(v, edge)[edge * stride : (edge + tile) * stride].reshape(tile, stride, chans)[:, :tile]
        htile[...] = mid(hid).astype(BF16)
        ctile[...] = mid(cell)
        store_h = pltpu.make_async_copy(htile, hout_ref.at[0, batch], sems.at[0])
        store_c = pltpu.make_async_copy(ctile, cout_ref.at[0, batch], sems.at[1])
        store_h.start()
        store_c.start()
        store_h.wait()
        store_c.wait()


def layer(tick, batch, tile, sec, x, hid, cell, w, b, mask, outs):
    stride = tile + 8
    rows = (tile + 2 * (3 - tick)) * stride
    first = outs is None
    vmem = pl.BlockSpec(memory_space=pltpu.VMEM)
    any_ = pl.BlockSpec(memory_space=pl.ANY)
    args = [sec, x, hid, cell, w, b, mask] + ([] if first else list(outs))
    shape_h = jax.ShapeDtypeStruct((1, 2, tile, tile, 128), BF16)
    shape_c = jax.ShapeDtypeStruct((1, 2, tile, tile, 128), F32)
    hout, cout, send = pl.pallas_call(
        functools.partial(layer_kernel, tick, batch, stride, tile, 3, first),
        out_shape=(shape_h, shape_c, jax.ShapeDtypeStruct((rows, 128), BF16)),
        in_specs=[pl.BlockSpec(memory_space=pltpu.SMEM)] + [vmem] * 6 + [any_] * (len(args) - 7),
        out_specs=(any_, any_, vmem),
        scratch_shapes=[
            pltpu.VMEM((rows, 18 * 128), BF16),
            pltpu.VMEM((tile, tile, 128), BF16),
            pltpu.VMEM((tile, tile, 128), F32),
            pltpu.SemaphoreType.DMA((2,)),
        ],
        input_output_aliases={} if first else {7: 0, 8: 1},
        compiler_params=pltpu.CompilerParams(vmem_limit_bytes=24 << 20),
        cost_estimate=pl.CostEstimate(
            flops=2 * rows * 2304 * 512, bytes_accessed=4 << 20, transcendentals=rows * 640
        ),
        name=f"layer_{tick}_{batch}",
    )(*args)
    return (hout, cout), send


def exchanged(x, axis, up):
    count = lax.axis_size(axis)
    pairs = [(i, i + 1) for i in range(count - 1)]
    return lax.ppermute(x, axis, pairs if up else [(j, i) for i, j in pairs])


def on_device(latent, hidden_old, cell_old, weights, bias):
    tile = latent.shape[1]
    wide = 4
    sec = lax.axis_index("section")
    row = lax.axis_index("row")
    col = lax.axis_index("col")
    hid = hidden_old[0]
    cell = cell_old[0]

    def stacked(rows, cols):
        return jnp.concatenate(
            [latent[:, rows, cols], hid[:, rows, cols], cell[:, rows, cols].astype(BF16)], axis=-1
        )

    everything, low, high = slice(None), slice(0, wide), slice(tile - wide, tile)
    left = exchanged(stacked(everything, high), "col", True)
    right = exchanged(stacked(everything, low), "col", False)
    ends = lambda part: jnp.concatenate([left[:, part], stacked(part, everything), right[:, part]], axis=2)
    above = exchanged(ends(high), "row", True)
    below = exchanged(ends(low), "row", False)

    def whole(k, own):
        part = slice(128 * k, 128 * (k + 1))
        grab = lambda v: v[..., part].astype(own.dtype)
        mid = jnp.concatenate([grab(left), own, grab(right)], axis=2)
        full = jnp.concatenate([grab(above), mid, grab(below)], axis=1)
        return full.reshape(2, -1, 128)

    full_in, full_hid, full_cell = whole(0, latent), whole(1, hid), whole(2, cell)
    stride = tile + 2 * wide
    w = weights.reshape(-1, weights.shape[-1])
    sec_arr = sec.reshape(1).astype(jnp.int32)
    total_r = tile * lax.axis_size("row")
    total_c = tile * lax.axis_size("col")

    def mask(tick):
        edge = 3 - tick
        count = tile + 2 * edge
        r = row * tile - edge + lax.broadcasted_iota(jnp.int32, (count, stride, 128), 0)
        c = col * tile - edge + lax.broadcasted_iota(jnp.int32, (count, stride, 128), 1)
        inside = (r >= 0) & (r < total_r) & (c >= 0) & (c < total_c)
        return inside.astype(F32).reshape(-1, 128)

    outs = None
    xs = [full_in, full_in]
    for tick in range(4):
        m = mask(tick)
        nxt = []
        for batch in range(2):
            outs, send = layer(tick, batch, tile, sec_arr, xs[batch], full_hid, full_cell, w, bias, m, outs)
            if tick < 3:
                nxt.append(lax.ppermute(send, "section", [(tick, tick + 1)]))
        xs = nxt
    return outs


def solution(mesh):
    in_specs = (
        P(None, "row", "col", None),
        P("section", None, "row", "col", None),
        P("section", None, "row", "col", None),
        P("section", None, None, None),
        P("section", None),
    )
    out_specs = (P("section", None, "row", "col", None), P("section", None, "row", "col", None))
    return jax.shard_map(
        on_device, mesh=mesh, in_specs=in_specs, out_specs=out_specs, check_vma=False
    )
```

```python
import functools

import jax
import jax.numpy as jnp
from jax import lax
from jax.experimental import pallas as pl
from jax.experimental.pallas import tpu as pltpu
from jax.sharding import PartitionSpec as P

F32 = jnp.float32
BF16 = jnp.bfloat16
CH = 128
LAYERS = 4
WIDE = 4
VMEM = pl.BlockSpec(memory_space=pltpu.VMEM)
SMEM = pl.BlockSpec(memory_space=pltpu.SMEM)
ANY = pl.BlockSpec(memory_space=pl.ANY)


def sigmoid(x):
    return 0.5 * jnp.tanh(0.5 * x) + 0.5


def rolled(x, by):
    rows = x.shape[0]
    by = by % rows
    return x if by == 0 else pltpu.roll(x, rows - by, 0)


def swap_halves(x):
    tiles = x.shape[0]
    flat = x.reshape(tiles * 8, CH)
    up, down = pltpu.roll(flat, 4, 0), pltpu.roll(flat, tiles * 8 - 4, 0)
    return jnp.where(top_half(flat.shape), down, up).reshape(x.shape)


def top_half(shape):
    return lax.broadcasted_iota(jnp.int32, shape, len(shape) - 2) % 8 < 4


def call(kernel, ins, in_specs, outs, out_specs, scratch=(), aliases=None, name=None, flops=0, limit=16):
    return pl.pallas_call(
        kernel,
        out_shape=tuple(outs),
        in_specs=in_specs,
        out_specs=tuple(out_specs),
        scratch_shapes=list(scratch),
        input_output_aliases=aliases or {},
        compiler_params=pltpu.CompilerParams(vmem_limit_bytes=limit << 20),
        cost_estimate=pl.CostEstimate(flops=flops, bytes_accessed=1 << 20, transcendentals=0),
        name=name,
    )(*ins)


def pack_kernel(lat_ref, hid_ref, cell_ref, low_ref, high_ref):
    for k, ref in enumerate((lat_ref, hid_ref, cell_ref)):
        first, second = ref[0].astype(F32), ref[1].astype(F32)
        tile = first.shape[0]
        top = top_half((tile, 8, CH))
        lanes = slice(k * CH, (k + 1) * CH)
        low = jnp.where(top, first[:, :8], swap_halves(second[:, :8]))
        high = jnp.where(top, swap_halves(first[:, 8:]), second[:, 8:])
        low_ref[:, lanes] = low.reshape(tile * 8, CH).astype(BF16)
        high_ref[:, lanes] = high.reshape(tile * 8, CH).astype(BF16)


def middle(own, left, right, batch):
    tile = own.shape[0]
    left, right = (v.astype(F32).reshape(tile, 8, CH) for v in (left, right))
    if batch == 0:
        left = swap_halves(left)
    else:
        right = swap_halves(right)
    top = top_half((tile, 8, CH))
    zero = jnp.zeros((1, 8, CH), F32)
    side = jnp.where(top, right, jnp.concatenate([left[1:], zero], axis=0))
    rows = jnp.concatenate([own, side], axis=1).reshape(tile * (tile + 8), CH)
    return jnp.concatenate([left[0], rows], axis=0)


def middle_kernel(where_ref, lat_ref, hid_ref, cell_ref, left_ref, right_ref, far_ref, near_ref):
    odd = where_ref[1] == 1
    for batch in range(2):
        for k, ref in enumerate((lat_ref, hid_ref, cell_ref)):
            lanes = slice(k * CH, (k + 1) * CH)
            mid = middle(ref[batch].astype(F32), left_ref[:, lanes], right_ref[:, lanes], batch)
            up, down = mid[:104].astype(BF16), mid[288:].astype(BF16)
            rows = slice(104 * batch, 104 * (batch + 1))

            @pl.when(odd)
            def _():
                far_ref[rows, lanes] = down
                near_ref[rows, lanes] = up

            @pl.when(jnp.logical_not(odd))
            def _():
                far_ref[rows, lanes] = up
                near_ref[rows, lanes] = down


def taps(src, at, cols_ref, rows, stride, step, first):
    for dx in range(3):
        moved = rolled(src, at + dx)
        for dy in range(3):
            lane = (3 * dy + dx) * step + first
            start = dy * stride
            cols_ref[:rows, lane : lane + CH] = moved[start : start + rows].astype(BF16)


def activated(gates, cell_prev):
    cell = sigmoid(gates[:, CH : 2 * CH]) * cell_prev + sigmoid(gates[:, :CH]) * jnp.tanh(gates[:, 2 * CH : 3 * CH])
    return sigmoid(gates[:, 3 * CH :]) * jnp.tanh(cell), cell


def centre(v, edge, tile, stride):
    return rolled(v, edge)[edge * stride : (edge + tile) * stride].reshape(tile, stride, CH)[:, :tile]


def first_kernel(batch, blocks, where_ref, lat_ref, hid_ref, cell_ref, left_ref, right_ref, far_ref, near_ref,
                 w_ref, b_ref, m_ref, send_ref, htile_ref, ctile_ref, part_ref, prev_ref, win_ref, cols):
    tile = lat_ref.shape[1]
    stride = tile + 8
    sec = where_ref[0]
    odd = where_ref[1] == 1

    def full(k, ref):
        lanes = slice(k * CH, (k + 1) * CH)
        rows = slice(104 * batch, 104 * (batch + 1))
        far, near = far_ref[rows, lanes].astype(F32), near_ref[rows, lanes].astype(F32)
        above, below = jnp.where(odd, near, far), jnp.where(odd, far, near)
        mid = middle(ref[batch].astype(F32), left_ref[:, lanes], right_ref[:, lanes], batch)
        top = top_half((8, CH))
        return jnp.concatenate(
            [above[:96], jnp.where(top, above[96:], mid[:8]), mid[8:384], jnp.where(top, mid[384:], below[:8]), below[8:]],
            axis=0,
        )

    @pl.when(sec == 0)
    def _():
        rows = (tile + 6) * stride
        taps(full(0, lat_ref), WIDE, cols, rows, stride, 2 * CH, 0)
        taps(full(1, hid_ref), WIDE, cols, rows, stride, 2 * CH, CH)
        prev = rolled(full(2, cell_ref), WIDE + 1)[stride : stride + rows]
        size = rows // blocks
        hs, cs = [], []
        for k in range(blocks):
            part = slice(k * size, (k + 1) * size)
            gates = jnp.dot(cols[part, :], w_ref[...], preferred_element_type=F32) + b_ref[...]
            h, c = activated(gates, prev[part])
            hs.append(h * m_ref[part, :])
            cs.append(c)
        h, c = jnp.concatenate(hs, axis=0), jnp.concatenate(cs, axis=0)
        send_ref[...] = h.astype(BF16)
        htile_ref[...] = centre(h, 3, tile, stride).astype(BF16)
        ctile_ref[...] = centre(c, 3, tile, stride)

    for s in range(1, LAYERS):

        @pl.when(sec == s)
        def _():
            edge = 3 - s
            rows = (tile + 2 * edge) * stride
            hidden = full(1, hid_ref)[s * stride :]
            taps(hidden, WIDE + s, cols, rows, stride, CH, 0)
            prev_ref[:rows, :] = rolled(full(2, cell_ref), WIDE + 1 + s)[(s + 1) * stride : (s + 1) * stride + rows]
            own = jnp.concatenate([w_ref[(2 * t + 1) * CH : (2 * t + 2) * CH, :] for t in range(9)], axis=0)
            part_ref[:rows, :] = (
                jnp.dot(cols[:rows, : 9 * CH], own, preferred_element_type=F32) + b_ref[...]
            )
            for t in range(9):
                win_ref[t * CH : (t + 1) * CH, :] = w_ref[2 * t * CH : (2 * t + 1) * CH, :]


def next_kernel(tick, blocks, where_ref, x_ref, part_ref, prev_ref, win_ref, m_ref, *rest):
    last = tick == LAYERS - 1
    if last:
        batch, (_, _, hout_ref, cout_ref, cols, htile_ref, ctile_ref, sems) = rest[0], rest[1:]
    else:
        send_ref, htile_ref, ctile_ref, cols = rest
    tile = htile_ref.shape[0]
    stride = tile + 8
    edge = 3 - tick
    rows = (tile + 2 * edge) * stride

    @pl.when(where_ref[0] == tick)
    def _():
        taps(x_ref[...].astype(F32), 0, cols, rows, stride, CH, 0)
        size = rows // blocks
        hs, cs = [], []
        for k in range(blocks):
            part = slice(k * size, (k + 1) * size)
            gates = jnp.dot(cols[part, :], win_ref[...], preferred_element_type=F32) + part_ref[part, :]
            h, c = activated(gates, prev_ref[part, :])
            hs.append(h if last else h * m_ref[part, :])
            cs.append(c)
        h, c = jnp.concatenate(hs, axis=0), jnp.concatenate(cs, axis=0)
        if not last:
            send_ref[...] = h.astype(BF16)
        htile_ref[...] = centre(h, edge, tile, stride).astype(BF16)
        ctile_ref[...] = centre(c, edge, tile, stride)
        if last:
            copies = [
                pltpu.make_async_copy(htile_ref, hout_ref.at[0, batch], sems.at[0]),
                pltpu.make_async_copy(ctile_ref, cout_ref.at[0, batch], sems.at[1]),
            ]
            for copy in copies:
                copy.start()
            for copy in copies:
                copy.wait()


def last_kernel(batch, blocks, where_ref, x_ref, part_ref, prev_ref, win_ref, m_ref, *rest):
    next_kernel(LAYERS - 1, blocks, where_ref, x_ref, part_ref, prev_ref, win_ref, m_ref, batch, *rest)


def store_kernel(where_ref, *rest):
    tiles, (hout_ref, cout_ref, sems) = rest[:-3], rest[-3:]
    for tick in range(LAYERS - 1):

        @pl.when(where_ref[0] == tick)
        def _():
            copies = []
            for batch in range(2):
                h, c = tiles[4 * tick + 2 * batch : 4 * tick + 2 * batch + 2]
                copies.append(pltpu.make_async_copy(h, hout_ref.at[0, batch], sems.at[2 * batch]))
                copies.append(pltpu.make_async_copy(c, cout_ref.at[0, batch], sems.at[2 * batch + 1]))
            for copy in copies:
                copy.start()
            for copy in copies:
                copy.wait()


def on_device(latent, hidden_old, cell_old, weights, bias):
    tile = latent.shape[1]
    stride = tile + 8
    sec = lax.axis_index("section")
    row = lax.axis_index("row")
    col = lax.axis_index("col")
    n_row, n_col = lax.axis_size("row"), lax.axis_size("col")
    hid = hidden_old[0]
    cell = cell_old[0]
    w = weights.reshape(-1, weights.shape[-1])
    where = jnp.stack([sec, row % 2]).astype(jnp.int32)

    edge = 3 - sec
    r = row * tile - edge + lax.broadcasted_iota(jnp.int32, (tile + 6, stride, CH), 0)
    c = col * tile - edge + lax.broadcasted_iota(jnp.int32, (tile + 6, stride, CH), 1)
    inside = (r >= 0) & (r < n_row * tile) & (c >= 0) & (c < n_col * tile)
    mask = inside.astype(F32).reshape(-1, CH)

    vm = lambda shape, kind: pltpu.VMEM(shape, kind)
    low, high = call(
        pack_kernel, (latent, hid, cell), [VMEM] * 3, [vm((8 * tile, 3 * CH), BF16)] * 2, [VMEM] * 2, name="pack"
    )
    up = [(i, i + 1) for i in range(n_col - 1)]
    left = lax.ppermute(high, "col", up)
    right = lax.ppermute(low, "col", [(j, i) for i, j in up])

    far, near = call(
        middle_kernel,
        (where, latent, hid, cell, left, right),
        [SMEM] + [VMEM] * 5,
        [vm((208, 3 * CH), BF16)] * 2,
        [VMEM] * 2,
        name="middle",
    )
    odd = [(i, i + 1) for i in range(1, n_row - 1, 2)]
    even = [(i, i + 1) for i in range(0, n_row - 1, 2)]
    both = lambda pairs: pairs + [(j, i) for i, j in pairs]
    far = lax.ppermute(far, "row", both(odd))
    near = lax.ppermute(near, "row", both(even))

    most = (tile + 4) * stride
    xs, state, tiles = [], [], []
    for batch in range(2):
        send, htile, ctile, part, prev, win = call(
            functools.partial(first_kernel, batch, 3),
            (where, latent, hid, cell, left, right, far, near, w, bias, mask),
            [SMEM] + [VMEM] * 10,
            [
                vm(((tile + 6) * stride, CH), BF16),
                vm((tile, tile, CH), BF16),
                vm((tile, tile, CH), F32),
                vm((most, 4 * CH), F32),
                vm((most, CH), F32),
                vm((9 * CH, 4 * CH), BF16),
            ],
            [VMEM] * 6,
            [pltpu.VMEM(((tile + 6) * stride, 18 * CH), BF16)],
            name=f"first_{batch}",
            flops=2 * 528 * 2304 * 512,
        )
        xs.append(lax.ppermute(send, "section", [(0, 1)]))
        state.append((part, prev, win))
        tiles += [htile, ctile]

    for tick in range(1, LAYERS - 1):
        rows = (tile + 2 * (3 - tick)) * stride
        nxt = []
        for batch in range(2):
            send, htile, ctile = call(
                functools.partial(next_kernel, tick, 3),
                (where, xs[batch], *state[batch], mask),
                [SMEM] + [VMEM] * 5,
                [vm((rows, CH), BF16), vm((tile, tile, CH), BF16), vm((tile, tile, CH), F32)],
                [VMEM] * 3,
                [pltpu.VMEM((rows, 9 * CH), BF16)],
                name=f"layer_{tick}_{batch}",
                flops=2 * rows * 1152 * 512,
            )
            nxt.append(lax.ppermute(send, "section", [(tick, tick + 1)]))
            tiles += [htile, ctile]
        xs = nxt

    out_shapes = [
        jax.ShapeDtypeStruct((1, 2, tile, tile, CH), BF16),
        jax.ShapeDtypeStruct((1, 2, tile, tile, CH), F32),
    ]
    outs = call(
        store_kernel,
        (where, *tiles),
        [SMEM] + [VMEM] * len(tiles),
        out_shapes,
        [ANY, ANY],
        [pltpu.SemaphoreType.DMA((4,))],
        name="store",
    )
    for batch in range(2):
        rows = tile * stride
        outs = call(
            functools.partial(last_kernel, batch, 3),
            (where, xs[batch], *state[batch], mask, *outs),
            [SMEM] + [VMEM] * 5 + [ANY] * 2,
            out_shapes,
            [ANY, ANY],
            [
                pltpu.VMEM((rows, 9 * CH), BF16),
                pltpu.VMEM((tile, tile, CH), BF16),
                pltpu.VMEM((tile, tile, CH), F32),
                pltpu.SemaphoreType.DMA((2,)),
            ],
            aliases={6: 0, 7: 1},
            name=f"layer_3_{batch}",
            flops=2 * rows * 1152 * 512,
        )
    return tuple(outs)


def solution(mesh):
    in_specs = (
        P(None, "row", "col", None),
        P("section", None, "row", "col", None),
        P("section", None, "row", "col", None),
        P("section", None, None, None),
        P("section", None),
    )
    out_specs = (P("section", None, "row", "col", None), P("section", None, "row", "col", None))
    return jax.shard_map(
        on_device, mesh=mesh, in_specs=in_specs, out_specs=out_specs, check_vma=False
    )
```

```python
import functools

import jax
import jax.numpy as jnp
from jax import lax
from jax.experimental import pallas as pl
from jax.experimental.pallas import tpu as pltpu
from jax.sharding import PartitionSpec as P

F32 = jnp.float32
BF16 = jnp.bfloat16
CH = 128
LAYERS = 4
WIDE = 4
VMEM = pl.BlockSpec(memory_space=pltpu.VMEM)
ANY = pl.BlockSpec(memory_space=pl.ANY)


def sigmoid(x):
    return 0.5 * jnp.tanh(0.5 * x) + 0.5


def rolled(x, by):
    rows = x.shape[0]
    by = by % rows
    return x if by == 0 else pltpu.roll(x, rows - by, 0)


def swap_halves(x):
    tiles = x.shape[0]
    flat = x.reshape(tiles * 8, CH)
    up, down = pltpu.roll(flat, 4, 0), pltpu.roll(flat, tiles * 8 - 4, 0)
    return jnp.where(top_half(flat.shape), down, up).reshape(x.shape)


def top_half(shape):
    return lax.broadcasted_iota(jnp.int32, shape, len(shape) - 2) % 8 < 4


def call(kernel, ins, in_specs, outs, out_specs, scratch=(), aliases=None, name=None, flops=0, limit=16):
    return pl.pallas_call(
        kernel,
        out_shape=tuple(outs),
        in_specs=in_specs,
        out_specs=tuple(out_specs),
        scratch_shapes=list(scratch),
        input_output_aliases=aliases or {},
        compiler_params=pltpu.CompilerParams(vmem_limit_bytes=limit << 20),
        cost_estimate=pl.CostEstimate(flops=flops, bytes_accessed=1 << 20, transcendentals=0),
        name=name,
    )(*ins)


def pack_kernel(lat_hbm, hid_hbm, cell_hbm, lat_ref, hid_ref, cell_ref, far_ref, near_ref, sems):
    odd = lax.axis_index("col") % 2 == 1
    copies = [
        pltpu.make_async_copy(src, dst, sems.at[k])
        for k, (src, dst) in enumerate(((lat_hbm, lat_ref), (hid_hbm, hid_ref), (cell_hbm, cell_ref)))
    ]
    for copy in copies:
        copy.start()
    for k, ref in enumerate((lat_ref, hid_ref, cell_ref)):
        copies[k].wait()
        first, second = ref[0].astype(F32), ref[1].astype(F32)
        tile = first.shape[0]
        top = top_half((tile, 8, CH))
        lanes = slice(k * CH, (k + 1) * CH)
        low = jnp.where(top, first[:, :8], swap_halves(second[:, :8]))
        high = jnp.where(top, swap_halves(first[:, 8:]), second[:, 8:])
        low, high = (v.reshape(tile * 8, CH).astype(BF16) for v in (low, high))

        @pl.when(odd)
        def _():
            far_ref[:, lanes] = high
            near_ref[:, lanes] = low

        @pl.when(jnp.logical_not(odd))
        def _():
            far_ref[:, lanes] = low
            near_ref[:, lanes] = high


def load_kernel(tile, _, w_hbm, b_hbm, w_ref, b_ref, win_ref, m_ref, sems):
    copies = [pltpu.make_async_copy(w_hbm, w_ref, sems.at[0]), pltpu.make_async_copy(b_hbm, b_ref, sems.at[1])]
    for copy in copies:
        copy.start()
    edge = 3 - lax.axis_index("section")
    shape = (tile + 6, tile + 8, CH)
    r = lax.axis_index("row") * tile - edge + lax.broadcasted_iota(jnp.int32, shape, 0)
    c = lax.axis_index("col") * tile - edge + lax.broadcasted_iota(jnp.int32, shape, 1)
    high, wide = lax.axis_size("row") * tile, lax.axis_size("col") * tile
    inside = (r >= 0) & (r < high) & (c >= 0) & (c < wide)
    m_ref[...] = jnp.where(inside, jnp.ones(shape, F32), jnp.zeros(shape, F32)).reshape(-1, CH)
    for copy in copies:
        copy.wait()

    @pl.when(lax.axis_index("section") > 0)
    def _():
        for t in range(9):
            win_ref[t * CH : (t + 1) * CH, :] = w_ref[2 * t * CH : (2 * t + 1) * CH, :]


def middle(own, far, near, batch):
    tile = own.shape[0]
    far, near = (v.astype(F32).reshape(tile, 8, CH) for v in (far, near))
    odd = lax.axis_index("col") % 2 == 1
    left, right = jnp.where(odd, near, far), jnp.where(odd, far, near)
    if batch == 0:
        left = swap_halves(left)
    else:
        right = swap_halves(right)
    top = top_half((tile, 8, CH))
    zero = jnp.zeros((1, 8, CH), F32)
    side = jnp.where(top, right, jnp.concatenate([left[1:], zero], axis=0))
    rows = jnp.concatenate([own, side], axis=1).reshape(tile * (tile + 8), CH)
    return jnp.concatenate([left[0], rows], axis=0)


def middle_kernel(lat_ref, hid_ref, cell_ref, left_ref, right_ref, _, far_ref, near_ref):
    odd = lax.axis_index("row") % 2 == 1
    for batch in range(2):
        for k, ref in enumerate((lat_ref, hid_ref, cell_ref)):
            lanes = slice(k * CH, (k + 1) * CH)
            mid = middle(ref[batch].astype(F32), left_ref[:, lanes], right_ref[:, lanes], batch)
            up, down = mid[:104].astype(BF16), mid[288:].astype(BF16)
            rows = slice(104 * batch, 104 * (batch + 1))

            @pl.when(odd)
            def _():
                far_ref[rows, lanes] = down
                near_ref[rows, lanes] = up

            @pl.when(jnp.logical_not(odd))
            def _():
                far_ref[rows, lanes] = up
                near_ref[rows, lanes] = down


def taps(src, at, cols_ref, rows, stride, step, first):
    for dx in range(3):
        moved = rolled(src, at + dx)
        for dy in range(3):
            lane = (3 * dy + dx) * step + first
            start = dy * stride
            cols_ref[:rows, lane : lane + CH] = moved[start : start + rows].astype(BF16)


def activated(gates, cell_prev):
    cell = sigmoid(gates[:, CH : 2 * CH]) * cell_prev + sigmoid(gates[:, :CH]) * jnp.tanh(gates[:, 2 * CH : 3 * CH])
    return sigmoid(gates[:, 3 * CH :]) * jnp.tanh(cell), cell


def centre(v, edge, tile, stride):
    return rolled(v, edge)[edge * stride : (edge + tile) * stride].reshape(tile, stride, CH)[:, :tile]


def first_kernel(batch, blocks, lat_ref, hid_ref, cell_ref, left_ref, right_ref, far_ref, near_ref,
                 w_ref, b_ref, m_ref, send_ref, htile_ref, ctile_ref, part_ref, prev_ref, cols):
    tile = lat_ref.shape[1]
    stride = tile + 8
    sec = lax.axis_index("section")
    odd = lax.axis_index("row") % 2 == 1

    def full(k, ref):
        lanes = slice(k * CH, (k + 1) * CH)
        rows = slice(104 * batch, 104 * (batch + 1))
        far, near = far_ref[rows, lanes].astype(F32), near_ref[rows, lanes].astype(F32)
        above, below = jnp.where(odd, near, far), jnp.where(odd, far, near)
        mid = middle(ref[batch].astype(F32), left_ref[:, lanes], right_ref[:, lanes], batch)
        top = top_half((8, CH))
        return jnp.concatenate(
            [above[:96], jnp.where(top, above[96:], mid[:8]), mid[8:384], jnp.where(top, mid[384:], below[:8]), below[8:]],
            axis=0,
        )

    @pl.when(sec == 0)
    def _():
        rows = (tile + 6) * stride
        taps(full(0, lat_ref), WIDE, cols, rows, stride, 2 * CH, 0)
        taps(full(1, hid_ref), WIDE, cols, rows, stride, 2 * CH, CH)
        prev = rolled(full(2, cell_ref), WIDE + 1)[stride : stride + rows]
        size = rows // blocks
        hs, cs = [], []
        for k in range(blocks):
            part = slice(k * size, (k + 1) * size)
            gates = jnp.dot(cols[part, :], w_ref[...], preferred_element_type=F32) + b_ref[...]
            h, c = activated(gates, prev[part])
            hs.append(h * m_ref[part, :])
            cs.append(c)
        h, c = jnp.concatenate(hs, axis=0), jnp.concatenate(cs, axis=0)
        send_ref[...] = h.astype(BF16)
        htile_ref[...] = centre(h, 3, tile, stride).astype(BF16)
        ctile_ref[...] = centre(c, 3, tile, stride)

    for s in range(1, LAYERS):

        @pl.when(sec == s)
        def _():
            edge = 3 - s
            rows = (tile + 2 * edge) * stride
            hidden = full(1, hid_ref)[s * stride :]
            taps(hidden, WIDE + s, cols, rows, stride, CH, 0)
            prev_ref[:rows, :] = rolled(full(2, cell_ref), WIDE + 1 + s)[(s + 1) * stride : (s + 1) * stride + rows]
            own = jnp.concatenate([w_ref[(2 * t + 1) * CH : (2 * t + 2) * CH, :] for t in range(9)], axis=0)
            part_ref[:rows, :] = (
                jnp.dot(cols[:rows, : 9 * CH], own, preferred_element_type=F32) + b_ref[...]
            )


def next_kernel(tick, blocks, x_ref, part_ref, prev_ref, win_ref, m_ref, *rest):
    last = tick == LAYERS - 1
    if last:
        batch, (_, _, hout_ref, cout_ref, cols, htile_ref, ctile_ref, sems) = rest[0], rest[1:]
    else:
        send_ref, htile_ref, ctile_ref, cols = rest
    tile = htile_ref.shape[0]
    stride = tile + 8
    edge = 3 - tick
    rows = (tile + 2 * edge) * stride

    @pl.when(lax.axis_index("section") == tick)
    def _():
        taps(x_ref[...].astype(F32), 0, cols, rows, stride, CH, 0)
        size = rows // blocks
        hs, cs = [], []
        for k in range(blocks):
            part = slice(k * size, (k + 1) * size)
            gates = jnp.dot(cols[part, :], win_ref[...], preferred_element_type=F32) + part_ref[part, :]
            h, c = activated(gates, prev_ref[part, :])
            hs.append(h if last else h * m_ref[part, :])
            cs.append(c)
        h, c = jnp.concatenate(hs, axis=0), jnp.concatenate(cs, axis=0)
        if not last:
            send_ref[...] = h.astype(BF16)
        htile_ref[...] = centre(h, edge, tile, stride).astype(BF16)
        ctile_ref[...] = centre(c, edge, tile, stride)
        if last:
            copies = [
                pltpu.make_async_copy(htile_ref, hout_ref.at[0, batch], sems.at[0]),
                pltpu.make_async_copy(ctile_ref, cout_ref.at[0, batch], sems.at[1]),
            ]
            for copy in copies:
                copy.start()
            for copy in copies:
                copy.wait()


def last_kernel(batch, blocks, x_ref, part_ref, prev_ref, win_ref, m_ref, *rest):
    next_kernel(LAYERS - 1, blocks, x_ref, part_ref, prev_ref, win_ref, m_ref, batch, *rest)


def store_kernel(*rest):
    tiles, (hout_ref, cout_ref, sems) = rest[:-3], rest[-3:]
    for tick in range(LAYERS - 1):

        @pl.when(lax.axis_index("section") == tick)
        def _():
            copies = []
            for batch in range(2):
                h, c = tiles[4 * tick + 2 * batch : 4 * tick + 2 * batch + 2]
                copies.append(pltpu.make_async_copy(h, hout_ref.at[0, batch], sems.at[2 * batch]))
                copies.append(pltpu.make_async_copy(c, cout_ref.at[0, batch], sems.at[2 * batch + 1]))
            for copy in copies:
                copy.start()
            for copy in copies:
                copy.wait()


def on_device(latent, hidden_old, cell_old, weights, bias):
    tile = latent.shape[1]
    stride = tile + 8
    n_row, n_col = lax.axis_size("row"), lax.axis_size("col")
    stay = lambda v: pltpu.with_memory_space_constraint(v, pltpu.HBM)
    hid = hidden_old[0]
    cell = cell_old[0]
    w = weights.reshape(-1, weights.shape[-1])

    vm = lambda shape, kind: pltpu.VMEM(shape, kind)
    odd = lambda n: [(i, i + 1) for i in range(1, n - 1, 2)]
    even = lambda n: [(i, i + 1) for i in range(0, n - 1, 2)]
    both = lambda pairs: pairs + [(j, i) for i, j in pairs]
    lat, hid, cell, left, right = call(
        pack_kernel,
        (stay(latent), stay(hid), stay(cell)),
        [ANY] * 3,
        [vm(latent.shape, BF16), vm(hid.shape, BF16), vm(cell.shape, F32)] + [vm((8 * tile, 3 * CH), BF16)] * 2,
        [VMEM] * 5,
        [pltpu.SemaphoreType.DMA((3,))],
        name="pack",
    )
    w, b, win, mask = call(
        functools.partial(load_kernel, tile),
        (right, stay(w), stay(bias)),
        [VMEM, ANY, ANY],
        [vm(w.shape, BF16), vm(bias.shape, F32), vm((9 * CH, 4 * CH), BF16), vm(((tile + 6) * stride, CH), F32)],
        [VMEM] * 4,
        [pltpu.SemaphoreType.DMA((2,))],
        name="load",
        flops=1 << 31,
    )
    left = lax.ppermute(left, "col", both(odd(n_col)))
    right = lax.ppermute(right, "col", both(even(n_col)))

    far, near = call(
        middle_kernel,
        (lat, hid, cell, left, right, b),
        [VMEM] * 6,
        [vm((208, 3 * CH), BF16)] * 2,
        [VMEM] * 2,
        name="middle",
    )
    far = lax.ppermute(far, "row", both(odd(n_row)))
    near = lax.ppermute(near, "row", both(even(n_row)))

    most = (tile + 4) * stride
    xs, state, tiles = [], [], []
    for batch in range(2):
        send, htile, ctile, part, prev = call(
            functools.partial(first_kernel, batch, 3),
            (lat, hid, cell, left, right, far, near, w, b, mask),
            [VMEM] * 10,
            [
                vm(((tile + 6) * stride, CH), BF16),
                vm((tile, tile, CH), BF16),
                vm((tile, tile, CH), F32),
                vm((most, 4 * CH), F32),
                vm((most, CH), F32),
            ],
            [VMEM] * 5,
            [pltpu.VMEM(((tile + 6) * stride, 18 * CH), BF16)],
            name=f"first_{batch}",
            flops=2 * 528 * 2304 * 512,
        )
        xs.append(lax.ppermute(send, "section", [(0, 1)]))
        state.append((part, prev, win))
        tiles += [htile, ctile]

    for tick in range(1, LAYERS - 1):
        rows = (tile + 2 * (3 - tick)) * stride
        nxt = []
        for batch in range(2):
            send, htile, ctile = call(
                functools.partial(next_kernel, tick, 3),
                (xs[batch], *state[batch], mask),
                [VMEM] * 5,
                [vm((rows, CH), BF16), vm((tile, tile, CH), BF16), vm((tile, tile, CH), F32)],
                [VMEM] * 3,
                [pltpu.VMEM((rows, 9 * CH), BF16)],
                name=f"layer_{tick}_{batch}",
                flops=2 * rows * 1152 * 512,
            )
            nxt.append(lax.ppermute(send, "section", [(tick, tick + 1)]))
            tiles += [htile, ctile]
        xs = nxt

    out_shapes = [
        jax.ShapeDtypeStruct((1, 2, tile, tile, CH), BF16),
        jax.ShapeDtypeStruct((1, 2, tile, tile, CH), F32),
    ]
    outs = call(
        store_kernel,
        (*tiles,),
        [VMEM] * len(tiles),
        out_shapes,
        [ANY, ANY],
        [pltpu.SemaphoreType.DMA((4,))],
        name="store",
    )
    for batch in range(2):
        rows = tile * stride
        outs = call(
            functools.partial(last_kernel, batch, 3),
            (xs[batch], *state[batch], mask, *outs),
            [VMEM] * 5 + [ANY] * 2,
            out_shapes,
            [ANY, ANY],
            [
                pltpu.VMEM((rows, 9 * CH), BF16),
                pltpu.VMEM((tile, tile, CH), BF16),
                pltpu.VMEM((tile, tile, CH), F32),
                pltpu.SemaphoreType.DMA((2,)),
            ],
            aliases={5: 0, 6: 1},
            name=f"layer_3_{batch}",
            flops=2 * rows * 1152 * 512,
        )
    return tuple(outs)


def solution(mesh):
    in_specs = (
        P(None, "row", "col", None),
        P("section", None, "row", "col", None),
        P("section", None, "row", "col", None),
        P("section", None, None, None),
        P("section", None),
    )
    out_specs = (P("section", None, "row", "col", None), P("section", None, "row", "col", None))
    return jax.shard_map(
        on_device, mesh=mesh, in_specs=in_specs, out_specs=out_specs, check_vma=False
    )
```

```python
import functools

import jax
import jax.numpy as jnp
from jax import lax
from jax.experimental import pallas as pl
from jax.experimental.pallas import tpu as pltpu
from jax.sharding import PartitionSpec as P


F32 = jnp.float32
BF16 = jnp.bfloat16
CH = 128
LAYERS = 4
BLOCKS = 1
EDGE = 6
WIDE = 4
VMEM = pl.BlockSpec(memory_space=pltpu.VMEM)
ANY = pl.BlockSpec(memory_space=pl.ANY)


def sigmoid(x):
    return 0.5 * jnp.tanh(0.5 * x) + 0.5


def rolled(x, by):
    rows = x.shape[0]
    by = by % rows
    return x if by == 0 else pltpu.roll(x, rows - by, 0)


def swap_halves(x):
    tiles = x.shape[0]
    flat = x.reshape(tiles * 8, CH)
    up, down = pltpu.roll(flat, 4, 0), pltpu.roll(flat, tiles * 8 - 4, 0)
    return jnp.where(top_half(flat.shape), down, up).reshape(x.shape)


def top_half(shape):
    return lax.broadcasted_iota(jnp.int32, shape, len(shape) - 2) % 8 < 4


def call(kernel, ins, in_specs, outs, out_specs, scratch=(), aliases=None, flops=0, limit=16, after=None):
    body = kernel
    if after is not None:
        ins, in_specs = (*ins, after), [*in_specs, VMEM]
        body = lambda *refs: kernel(*refs[: len(ins) - 1], *refs[len(ins) :])
    return pl.pallas_call(
        body,
        out_shape=tuple(outs),
        in_specs=in_specs,
        out_specs=tuple(out_specs),
        scratch_shapes=list(scratch),
        input_output_aliases=aliases or {},
        compiler_params=pltpu.CompilerParams(vmem_limit_bytes=limit << 20),
        cost_estimate=pl.CostEstimate(flops=flops, bytes_accessed=1 << 20, transcendentals=0),
    )(*ins)


def pack_kernel(lat_hbm, hid_hbm, cell_hbm, lat_ref, hid_ref, cell_ref, far_ref, near_ref, sems):
    odd = lax.axis_index("col") % 2 == 1
    copies = [
        pltpu.make_async_copy(src, dst, sems.at[k])
        for k, (src, dst) in enumerate(((lat_hbm, lat_ref), (hid_hbm, hid_ref), (cell_hbm, cell_ref)))
    ]
    for copy in copies:
        copy.start()
    for k, ref in enumerate((lat_ref, hid_ref, cell_ref)):
        copies[k].wait()
        first, second = ref[0].astype(F32), ref[1].astype(F32)
        tile = first.shape[0]
        top = top_half((tile, 8, CH))
        lanes = slice(k * CH, (k + 1) * CH)
        low = jnp.where(top, first[:, :8], swap_halves(second[:, :8]))
        high = jnp.where(top, swap_halves(first[:, 8:]), second[:, 8:])
        low, high = (v.reshape(tile * 8, CH).astype(BF16) for v in (low, high))

        @pl.when(odd)
        def _():
            far_ref[:, lanes] = high
            near_ref[:, lanes] = low

        @pl.when(jnp.logical_not(odd))
        def _():
            far_ref[:, lanes] = low
            near_ref[:, lanes] = high


def load_kernel(tile, _, w_hbm, b_hbm, w_ref, b_ref, win_ref, m_ref, sems):
    copies = [pltpu.make_async_copy(w_hbm, w_ref, sems.at[0]), pltpu.make_async_copy(b_hbm, b_ref, sems.at[1])]
    for copy in copies:
        copy.start()
    edge = 3 - lax.axis_index("section")
    shape = (tile + 6, tile + 8, CH)
    r = lax.axis_index("row") * tile - edge + lax.broadcasted_iota(jnp.int32, shape, 0)
    c = lax.axis_index("col") * tile - edge + lax.broadcasted_iota(jnp.int32, shape, 1)
    high, wide = lax.axis_size("row") * tile, lax.axis_size("col") * tile
    inside = (r >= 0) & (r < high) & (c >= 0) & (c < wide)
    m_ref[...] = jnp.where(inside, jnp.ones(shape, F32), jnp.zeros(shape, F32)).reshape(-1, CH)
    for copy in copies:
        copy.wait()

    @pl.when(lax.axis_index("section") > 0)
    def _():
        for t in range(9):
            win_ref[t * CH : (t + 1) * CH, :] = w_ref[2 * t * CH : (2 * t + 1) * CH, :]


def middle(own, far, near, batch):
    tile = own.shape[0]
    far, near = (v.astype(F32).reshape(tile, 8, CH) for v in (far, near))
    odd = lax.axis_index("col") % 2 == 1
    left, right = jnp.where(odd, near, far), jnp.where(odd, far, near)
    if batch == 0:
        left = swap_halves(left)
    else:
        right = swap_halves(right)
    top = top_half((tile, 8, CH))
    zero = jnp.zeros((1, 8, CH), F32)
    side = jnp.where(top, right, jnp.concatenate([left[1:], zero], axis=0))
    rows = jnp.concatenate([own, side], axis=1).reshape(tile * (tile + 8), CH)
    return jnp.concatenate([left[0], rows], axis=0)


def middle_kernel(lat_ref, hid_ref, cell_ref, left_ref, right_ref, _, far_ref, near_ref):
    odd = lax.axis_index("row") % 2 == 1
    for batch in range(2):
        for k, ref in enumerate((lat_ref, hid_ref, cell_ref)):
            lanes = slice(k * CH, (k + 1) * CH)
            mid = middle(ref[batch].astype(F32), left_ref[:, lanes], right_ref[:, lanes], batch)
            up, down = mid[:104].astype(BF16), mid[288:].astype(BF16)
            rows = slice(104 * batch, 104 * (batch + 1))

            @pl.when(odd)
            def _():
                far_ref[rows, lanes] = down
                near_ref[rows, lanes] = up

            @pl.when(jnp.logical_not(odd))
            def _():
                far_ref[rows, lanes] = up
                near_ref[rows, lanes] = down


def taps(src, at, cols_ref, rows, stride, step, first, row=0):
    for dx in range(3):
        moved = rolled(src, at + dx)
        for dy in range(3):
            lane = (3 * dy + dx) * step + first
            start = dy * stride
            cols_ref[row : row + rows, lane : lane + CH] = moved[start : start + rows].astype(BF16)


def activated(gates, cell_prev):
    cell = sigmoid(gates[:, CH : 2 * CH]) * cell_prev + sigmoid(gates[:, :CH]) * jnp.tanh(gates[:, 2 * CH : 3 * CH])
    return sigmoid(gates[:, 3 * CH :]) * jnp.tanh(cell), cell


def updated(cols, blocks, weight, extra, prev, mask):
    rows = prev.shape[0]
    size = rows // blocks
    hs, cs = [], []
    for k in range(blocks):
        part = slice(k * size, (k + 1) * size)
        add = extra if extra.shape[0] == 1 else extra[part]
        h, c = activated(jnp.dot(cols[part, :], weight[...], preferred_element_type=F32) + add, prev[part])
        hs.append(h if mask is None else h * mask[part])
        cs.append(c)
    return jnp.concatenate(hs, axis=0), jnp.concatenate(cs, axis=0)


def trimmed(v, edge, tile, stride):
    return rolled(v, edge).reshape(v.shape[0] // stride, stride, CH)[:, :tile]


def edge_rows(v, edge, tile, stride):
    v = trimmed(v, edge, tile, stride)
    return jnp.concatenate([v[edge:EDGE], v[EDGE : 2 * EDGE - edge]], axis=0)


def outer(v, stride):
    return jnp.concatenate([v[: EDGE * stride], v[-EDGE * stride :]], axis=0)


def middle_of(batch, k, ref, left_ref, right_ref):
    lanes = slice(k * CH, (k + 1) * CH)
    return middle(ref[batch].astype(F32), left_ref[:, lanes], right_ref[:, lanes], batch)


def first_middle_kernel(blocks, lat_ref, hid_ref, cell_ref, left_ref, right_ref, w_ref, b_ref, m_ref,
                        send_ref, htile_ref, ctile_ref, cols):
    tile = lat_ref.shape[1]
    stride = tile + 8

    @pl.when(lax.axis_index("section") == 0)
    def _():
        rows = (tile + 6 - 2 * EDGE) * stride
        skip = (EDGE - WIDE) * stride
        prev = []
        for batch in range(2):
            for k, ref in enumerate((lat_ref, hid_ref)):
                src = middle_of(batch, k, ref, left_ref, right_ref)[skip:]
                taps(src, WIDE, cols, rows, stride, 2 * CH, k * CH, batch * rows)
            state = rolled(middle_of(batch, 2, cell_ref, left_ref, right_ref), WIDE + 1)
            prev.append(state[skip + stride : skip + stride + rows])
        mask = m_ref[EDGE * stride : EDGE * stride + rows, :]
        h, c = updated(cols, blocks, w_ref, b_ref[...], jnp.concatenate(prev), jnp.concatenate([mask, mask]))
        send_ref[...] = h.astype(BF16)
        for batch in range(2):
            own = slice(batch * rows, (batch + 1) * rows)
            htile_ref[batch] = trimmed(h[own], 3, tile, stride).astype(BF16)
            ctile_ref[batch] = trimmed(c[own], 3, tile, stride)


def own_weight(w_ref):
    return jnp.concatenate([w_ref[(2 * t + 1) * CH : (2 * t + 2) * CH, :] for t in range(9)], axis=0)


def bordered(k, ref, batch, left_ref, right_ref, far_ref, near_ref):
    odd = lax.axis_index("row") % 2 == 1
    lanes = slice(k * CH, (k + 1) * CH)
    rows = slice(104 * batch, 104 * (batch + 1))
    far, near = far_ref[rows, lanes].astype(F32), near_ref[rows, lanes].astype(F32)
    above, below = jnp.where(odd, near, far), jnp.where(odd, far, near)
    mid = middle(ref[batch].astype(F32), left_ref[:, lanes], right_ref[:, lanes], batch)
    top = top_half((8, CH))
    first = jnp.where(top, above[96:], mid[:8])
    last = jnp.where(top, mid[384:], below[:8])
    return above[:96], first, mid, last, below[8:]


def first_edge_kernel(blocks, lat_ref, hid_ref, cell_ref, left_ref, right_ref, far_ref, near_ref,
                      w_ref, b_ref, m_ref, _, mid_part_ref, mid_prev_ref, part_ref, prev_ref, *rest):
    sends, tiles, cols = rest[:2], rest[2:6], rest[6]
    tile = lat_ref.shape[1]
    stride = tile + 8
    size = EDGE * stride
    rows = 2 * size

    for s in range(LAYERS):

        @pl.when(lax.axis_index("section") == s)
        def _():
            step = 2 * CH if s == 0 else CH
            starts = (s * stride, (s + tile + 6 - 2 * s - EDGE) * stride)
            prev = []

            def full(batch, k, ref):
                above, first, mid, last, below = bordered(k, ref, batch, left_ref, right_ref, far_ref, near_ref)
                return jnp.concatenate([above, first, mid[8:384], last, below], axis=0)

            for batch in range(2):
                for k, ref in enumerate((lat_ref, hid_ref)):
                    if k == 0 and s > 0:
                        continue
                    whole = full(batch, k, ref)
                    lane = step - CH if k else 0
                    for half, start in enumerate(starts):
                        src = whole[start : min(start + size + 3 * stride, whole.shape[0])]
                        taps(src, WIDE + s, cols, size, stride, step, lane, batch * rows + half * size)
                state = rolled(full(batch, 2, cell_ref), WIDE + 1 + s)
                prev += [state[start + stride : start + stride + size] for start in starts]
            if s == 0:
                mask = outer(m_ref[...], stride)
                h, c = updated(cols, blocks, w_ref, b_ref[...], jnp.concatenate(prev), jnp.concatenate([mask, mask]))
                for batch in range(2):
                    own = slice(batch * rows, (batch + 1) * rows)
                    sends[batch][...] = h[own].astype(BF16)
                    tiles[2 * batch][...] = edge_rows(h[own], 3, tile, stride).astype(BF16)
                    tiles[2 * batch + 1][...] = edge_rows(c[own], 3, tile, stride)
            else:
                prev_ref[...] = jnp.concatenate(prev)
                inner = (tile + 6 - 2 * s - 2 * EDGE) * stride
                skip = (s + EDGE - WIDE) * stride
                for batch in range(2):
                    src = middle_of(batch, 1, hid_ref, left_ref, right_ref)[skip:]
                    taps(src, WIDE + s, cols, inner, stride, CH, 0, 2 * rows + batch * inner)
                    state = rolled(middle_of(batch, 2, cell_ref, left_ref, right_ref), WIDE + 1 + s)
                    mid_prev_ref[batch * inner : (batch + 1) * inner, :] = state[skip + stride : skip + stride + inner]
                total = 2 * rows + 2 * inner
                gates = (
                    jnp.dot(cols[:total, : 9 * CH], own_weight(w_ref), preferred_element_type=F32) + b_ref[...]
                )
                part_ref[...] = gates[: 2 * rows]
                mid_part_ref[: 2 * inner, :] = gates[2 * rows :]


def next_middle_kernel(tick, blocks, x_ref, part_ref, prev_ref, win_ref, m_ref, *rest):
    send_ref, (htile_ref, ctile_ref, cols) = rest[0], rest[-3:]
    tile = htile_ref.shape[2]
    stride = tile + 8
    rows = (tile + 6 - 2 * tick - 2 * EDGE) * stride
    taken = rows + 2 * stride

    @pl.when(lax.axis_index("section") == tick)
    def _():
        for batch in range(2):
            x = x_ref[batch * taken : (batch + 1) * taken, :].astype(F32)
            taps(x, 0, cols, rows, stride, CH, 0, batch * rows)
        mask = None
        if tick < LAYERS - 1:
            mask = m_ref[EDGE * stride : EDGE * stride + rows, :]
            mask = jnp.concatenate([mask, mask])
        h, c = updated(cols, blocks, win_ref, part_ref[: 2 * rows, :], prev_ref[: 2 * rows, :], mask)
        if tick < LAYERS - 1:
            send_ref[...] = h.astype(BF16)
        for batch in range(2):
            own = slice(batch * rows, (batch + 1) * rows)
            htile_ref[batch] = trimmed(h[own], 3 - tick, tile, stride).astype(BF16)
            ctile_ref[batch] = trimmed(c[own], 3 - tick, tile, stride)


def next_edge(tick, batch, blocks, tile, x_ref, inner_ref, part_ref, prev_ref, win_ref, m_ref, cols):
    stride = tile + 8
    size, two = EDGE * stride, 2 * stride
    taken = inner_ref.shape[0] // 2
    x, inner = x_ref[...].astype(F32), inner_ref[batch * taken : (batch + 1) * taken, :].astype(F32)
    taps(jnp.concatenate([x[:size], inner[:two]], axis=0), 0, cols, size, stride, CH, 0)
    taps(jnp.concatenate([inner[-two:], x[size:]], axis=0), 0, cols, size, stride, CH, 0, size)
    mask = None if tick == LAYERS - 1 else outer(m_ref[: (tile + 6 - 2 * tick) * stride, :], stride)
    own = slice(2 * size * batch, 2 * size * (batch + 1))
    return updated(cols, blocks, win_ref, part_ref[own, :], prev_ref[own, :], mask)


def next_edge_kernel(tick, batch, blocks, x_ref, inner_ref, part_ref, prev_ref, win_ref, m_ref,
                     send_ref, htile_ref, ctile_ref, cols):
    tile = htile_ref.shape[1]

    @pl.when(lax.axis_index("section") == tick)
    def _():
        h, c = next_edge(tick, batch, blocks, tile, x_ref, inner_ref, part_ref, prev_ref, win_ref, m_ref, cols)
        send_ref[...] = h.astype(BF16)
        htile_ref[...] = edge_rows(h, 3 - tick, tile, tile + 8).astype(BF16)
        ctile_ref[...] = edge_rows(c, 3 - tick, tile, tile + 8)


def stores(tick, batch, tile_ref, out_ref, sems, k):
    tile = out_ref.shape[2]
    part = EDGE - 3 + tick
    if batch is None:
        return [pltpu.make_async_copy(tile_ref, out_ref.at[0, :, pl.ds(part, tile - 2 * part)], sems.at[k])]
    return [
        pltpu.make_async_copy(tile_ref.at[pl.ds(0, part)], out_ref.at[0, batch, pl.ds(0, part)], sems.at[k]),
        pltpu.make_async_copy(
            tile_ref.at[pl.ds(part, part)], out_ref.at[0, batch, pl.ds(tile - part, part)], sems.at[k + 1]
        ),
    ]


def last_kernel(batch, blocks, x_ref, inner_ref, part_ref, prev_ref, win_ref, m_ref, *rest):
    done, (_, _, hout_ref, cout_ref, cols, htile_ref, ctile_ref, sems) = rest[:-8], rest[-8:]
    tick = LAYERS - 1
    tile = htile_ref.shape[1]

    @pl.when(lax.axis_index("section") == tick)
    def _():
        copies = []
        if batch == 0:
            copies += stores(tick, None, done[0], hout_ref, sems, 4) + stores(tick, None, done[1], cout_ref, sems, 5)
        for copy in copies:
            copy.start()
        h, c = next_edge(tick, batch, blocks, tile, x_ref, inner_ref, part_ref, prev_ref, win_ref, m_ref, cols)
        ctile_ref[...] = edge_rows(c, 0, tile, tile + 8)
        htile_ref[...] = edge_rows(h, 0, tile, tile + 8).astype(BF16)
        mine = stores(tick, batch, ctile_ref, cout_ref, sems, 0) + stores(tick, batch, htile_ref, hout_ref, sems, 2)
        for copy in mine:
            copy.start()
        for copy in copies + mine:
            copy.wait()


def store_kernel(*rest):
    tiles, (hout_ref, cout_ref, sems) = rest[:-3], rest[-3:]
    for tick in range(LAYERS - 1):

        @pl.when(lax.axis_index("section") == tick)
        def _():
            copies = []
            for n, batch in enumerate((None, 0, 1)):
                h, c = tiles[6 * tick + 2 * n : 6 * tick + 2 * n + 2]
                copies += stores(tick, batch, h, hout_ref, sems, 4 * n)
                copies += stores(tick, batch, c, cout_ref, sems, 4 * n + 2)
            for copy in copies:
                copy.start()
            for copy in copies:
                copy.wait()


def on_device(latent, hidden_old, cell_old, weights, bias):
    tile = latent.shape[1]
    stride = tile + 8
    n_row, n_col = lax.axis_size("row"), lax.axis_size("col")
    stay = lambda v: pltpu.with_memory_space_constraint(v, pltpu.HBM)
    hid = hidden_old[0]
    cell = cell_old[0]
    w = weights.reshape(-1, weights.shape[-1])

    vm = lambda shape, kind: pltpu.VMEM(shape, kind)
    odd = lambda n: [(i, i + 1) for i in range(1, n - 1, 2)]
    even = lambda n: [(i, i + 1) for i in range(0, n - 1, 2)]
    both = lambda pairs: pairs + [(j, i) for i, j in pairs]
    lat, hid, cell, left, right = call(
        pack_kernel,
        (stay(latent), stay(hid), stay(cell)),
        [ANY] * 3,
        [vm(latent.shape, BF16), vm(hid.shape, BF16), vm(cell.shape, F32)] + [vm((8 * tile, 3 * CH), BF16)] * 2,
        [VMEM] * 5,
        [pltpu.SemaphoreType.DMA((3,))],
    )
    w, b, win, mask = call(
        functools.partial(load_kernel, tile),
        (right, stay(w), stay(bias)),
        [VMEM, ANY, ANY],
        [vm(w.shape, BF16), vm(bias.shape, F32), vm((9 * CH, 4 * CH), BF16), vm(((tile + 6) * stride, CH), F32)],
        [VMEM] * 4,
        [pltpu.SemaphoreType.DMA((2,))],
        flops=1 << 31,
    )
    left = lax.ppermute(left, "col", both(odd(n_col)))
    right = lax.ppermute(right, "col", both(even(n_col)))

    far, near = call(
        middle_kernel, (lat, hid, cell, left, right, b), [VMEM] * 6, [vm((208, 3 * CH), BF16)] * 2, [VMEM] * 2
    )
    far = lax.ppermute(far, "row", both(odd(n_row)))
    near = lax.ppermute(near, "row", both(even(n_row)))

    def height(tick):
        return tile + 6 - 2 * tick - 2 * EDGE

    def tiles_of(tick, kind):
        part = EDGE - 3 + tick
        shape = (2 * part, tile, CH) if kind else (2, tile - 2 * part, tile, CH)
        return [vm(shape, BF16), vm(shape, F32)]

    def hop(v, tick):
        return lax.ppermute(v, "section", [(tick, tick + 1)])

    edge = 2 * EDGE * stride
    rows = 2 * height(0) * stride
    send, htile, ctile = call(
        functools.partial(first_middle_kernel, BLOCKS),
        (lat, hid, cell, left, right, w, b, mask),
        [VMEM] * 8,
        [vm((rows, CH), BF16)] + tiles_of(0, 0),
        [VMEM] * 3,
        [pltpu.VMEM((rows, 18 * CH), BF16)],
        flops=2 * rows * 2304 * 512,
    )
    xs, tiles = [hop(send, 0)], [htile, ctile]
    inner = 2 * height(1) * stride
    *state, first, second, h0, c0, h1, c1 = call(
        functools.partial(first_edge_kernel, BLOCKS),
        (lat, hid, cell, left, right, far, near, w, b, mask, htile),
        [VMEM] * 11,
        [vm((rows, width), F32) for rows in (inner, 2 * edge) for width in (4 * CH, CH)]
        + [vm((edge, CH), BF16)] * 2
        + tiles_of(0, 1) * 2,
        [VMEM] * 10,
        [pltpu.VMEM((2 * edge + inner, 18 * CH), BF16)],
        flops=4 * edge * 2304 * 512,
    )
    state = (state[:2], state[2:])
    xs += [hop(first, 0), hop(second, 0)]
    tiles += [h0, c0, h1, c1]

    out_shapes = [
        jax.ShapeDtypeStruct((1, 2, tile, tile, CH), BF16),
        jax.ShapeDtypeStruct((1, 2, tile, tile, CH), F32),
    ]
    for tick in range(1, LAYERS):
        last = tick == LAYERS - 1
        rows = 2 * height(tick) * stride
        result = call(
            functools.partial(next_middle_kernel, tick, BLOCKS),
            (xs[0], *state[0], win, mask),
            [VMEM] * 5,
            ([] if last else [vm((rows, CH), BF16)]) + tiles_of(tick, 0),
            [VMEM] * (2 if last else 3),
            [pltpu.VMEM((rows, 9 * CH), BF16)],
            flops=2 * rows * 1152 * 512,
        )
        mine = list(result[-2:])
        nxt = [] if last else [hop(result[0], tick)]
        for batch in range(2):
            ins = (xs[1 + batch], xs[0], *state[1], win, mask)
            cols = pltpu.VMEM((edge, 9 * CH), BF16)
            if last:
                done = tuple(mine) if batch == 0 else ()
                count = len(ins) + len(done)
                outs = call(
                    functools.partial(last_kernel, batch, BLOCKS),
                    (*ins, *done, *outs),
                    [VMEM] * count + [ANY] * 2,
                    out_shapes,
                    [ANY, ANY],
                    [cols] + tiles_of(tick, 1) + [pltpu.SemaphoreType.DMA((6,))],
                    aliases={count: 0, count + 1: 1},
                    flops=2 * edge * 1152 * 512,
                )
                continue
            send, *result = call(
                functools.partial(next_edge_kernel, tick, batch, BLOCKS),
                ins,
                [VMEM] * len(ins),
                [vm((edge, CH), BF16)] + tiles_of(tick, 1),
                [VMEM] * 3,
                [cols],
                flops=2 * edge * 1152 * 512,
                after=mine[-2],
            )
            mine += result
            nxt.append(hop(send, tick))
        xs = nxt
        tiles += mine
        if tick == LAYERS - 2:
            outs = call(
                store_kernel, (*tiles,), [VMEM] * len(tiles), out_shapes, [ANY, ANY], [pltpu.SemaphoreType.DMA((12,))]
            )
    return tuple(outs)


def solution(mesh):
    in_specs = (
        P(None, "row", "col", None),
        P("section", None, "row", "col", None),
        P("section", None, "row", "col", None),
        P("section", None, None, None),
        P("section", None),
    )
    out_specs = (P("section", None, "row", "col", None), P("section", None, "row", "col", None))

    return jax.shard_map(on_device, mesh=mesh, in_specs=in_specs, out_specs=out_specs, check_vma=False)
```

```python
import functools

import jax
import jax.numpy as jnp
from jax import lax
from jax.experimental import pallas as pl
from jax.experimental.pallas import tpu as pltpu
from jax.sharding import PartitionSpec as P


F32 = jnp.float32
BF16 = jnp.bfloat16
CH = 128
LAYERS = 4
BLOCKS = 1
EDGE = 6
WIDE = 4
VMEM = pl.BlockSpec(memory_space=pltpu.VMEM)
ANY = pl.BlockSpec(memory_space=pl.ANY)


def sigmoid(x):
    return 0.5 * jnp.tanh(0.5 * x) + 0.5


def rolled(x, by):
    rows = x.shape[0]
    by = by % rows
    return x if by == 0 else pltpu.roll(x, rows - by, 0)


def swap_halves(x):
    tiles = x.shape[0]
    flat = x.reshape(tiles * 8, CH)
    up, down = pltpu.roll(flat, 4, 0), pltpu.roll(flat, tiles * 8 - 4, 0)
    return jnp.where(top_half(flat.shape), down, up).reshape(x.shape)


def top_half(shape):
    return lax.broadcasted_iota(jnp.int32, shape, len(shape) - 2) % 8 < 4


def call(kernel, ins, in_specs, outs, out_specs, scratch=(), aliases=None, flops=0, limit=16, after=None):
    body = kernel
    if after is not None:
        ins, in_specs = (*ins, after), [*in_specs, VMEM]
        body = lambda *refs: kernel(*refs[: len(ins) - 1], *refs[len(ins) :])
    return pl.pallas_call(
        body,
        out_shape=tuple(outs),
        in_specs=in_specs,
        out_specs=tuple(out_specs),
        scratch_shapes=list(scratch),
        input_output_aliases=aliases or {},
        compiler_params=pltpu.CompilerParams(vmem_limit_bytes=limit << 20),
        cost_estimate=pl.CostEstimate(flops=flops, bytes_accessed=1 << 20, transcendentals=0),
    )(*ins)


def pack_kernel(lat_hbm, hid_hbm, cell_hbm, lat_ref, hid_ref, cell_ref, far_ref, near_ref, sems):
    odd = lax.axis_index("col") % 2 == 1
    copies = [
        pltpu.make_async_copy(src, dst, sems.at[k])
        for k, (src, dst) in enumerate(((lat_hbm, lat_ref), (hid_hbm, hid_ref), (cell_hbm, cell_ref)))
    ]
    for copy in copies:
        copy.start()
    for k, ref in enumerate((lat_ref, hid_ref, cell_ref)):
        copies[k].wait()
        first, second = ref[0].astype(F32), ref[1].astype(F32)
        tile = first.shape[0]
        top = top_half((tile, 8, CH))
        lanes = slice(k * CH, (k + 1) * CH)
        low = jnp.where(top, first[:, :8], swap_halves(second[:, :8]))
        high = jnp.where(top, swap_halves(first[:, 8:]), second[:, 8:])
        low, high = (v.reshape(tile * 8, CH).astype(BF16) for v in (low, high))

        @pl.when(odd)
        def _():
            far_ref[:, lanes] = high
            near_ref[:, lanes] = low

        @pl.when(jnp.logical_not(odd))
        def _():
            far_ref[:, lanes] = low
            near_ref[:, lanes] = high


def load_kernel(tile, _, w_hbm, b_hbm, w_ref, b_ref, win_ref, m_ref, sems):
    copies = [pltpu.make_async_copy(w_hbm, w_ref, sems.at[0]), pltpu.make_async_copy(b_hbm, b_ref, sems.at[1])]
    for copy in copies:
        copy.start()
    high, width = lax.axis_size("row") * tile, lax.axis_size("col") * tile
    for s in range(LAYERS - 1):

        @pl.when(lax.axis_index("section") == s)
        def _():
            n = tile + 6 - 2 * s
            shape = (n, tile + 8, CH)
            r = lax.axis_index("row") * tile - (3 - s) + lax.broadcasted_iota(jnp.int32, shape, 0)
            c = lax.axis_index("col") * tile - (3 - s) + lax.broadcasted_iota(jnp.int32, shape, 1)
            inside = (r >= 0) & (r < high) & (c >= 0) & (c < width)
            wide = jnp.where(inside, jnp.ones(shape, F32), jnp.zeros(shape, F32))
            m_ref[n * n :, :] = jnp.zeros((m_ref.shape[0] - n * n, CH), F32)
            for k in range(n):
                m_ref[k * n : (k + 1) * n, :] = wide[k][:n]

    for copy in copies:
        copy.wait()

    @pl.when(lax.axis_index("section") > 0)
    def _():
        for t in range(9):
            win_ref[t * CH : (t + 1) * CH, :] = w_ref[2 * t * CH : (2 * t + 1) * CH, :]


def middle(own, far, near, batch):
    tile = own.shape[0]
    far, near = (v.astype(F32).reshape(tile, 8, CH) for v in (far, near))
    odd = lax.axis_index("col") % 2 == 1
    left, right = jnp.where(odd, near, far), jnp.where(odd, far, near)
    if batch == 0:
        left = swap_halves(left)
    else:
        right = swap_halves(right)
    top = top_half((tile, 8, CH))
    zero = jnp.zeros((1, 8, CH), F32)
    side = jnp.where(top, right, jnp.concatenate([left[1:], zero], axis=0))
    rows = jnp.concatenate([own, side], axis=1).reshape(tile * (tile + 8), CH)
    return jnp.concatenate([left[0], rows], axis=0)


def middle_kernel(lat_ref, hid_ref, cell_ref, left_ref, right_ref, _, far_ref, near_ref):
    odd = lax.axis_index("row") % 2 == 1
    for batch in range(2):
        for k, ref in enumerate((lat_ref, hid_ref, cell_ref)):
            lanes = slice(k * CH, (k + 1) * CH)
            mid = middle(ref[batch].astype(F32), left_ref[:, lanes], right_ref[:, lanes], batch)
            up, down = mid[:104].astype(BF16), mid[288:].astype(BF16)
            rows = slice(104 * batch, 104 * (batch + 1))

            @pl.when(odd)
            def _():
                far_ref[rows, lanes] = down
                near_ref[rows, lanes] = up

            @pl.when(jnp.logical_not(odd))
            def _():
                far_ref[rows, lanes] = up
                near_ref[rows, lanes] = down


def taps(src, at, cols_ref, rows, stride, step, first, row=0):
    for dx in range(3):
        moved = rolled(src, at + dx)
        for dy in range(3):
            lane = (3 * dy + dx) * step + first
            start = dy * stride
            cols_ref[row : row + rows, lane : lane + CH] = moved[start : start + rows].astype(BF16)


def activated(gates, cell_prev):
    cell = sigmoid(gates[:, CH : 2 * CH]) * cell_prev + sigmoid(gates[:, :CH]) * jnp.tanh(gates[:, 2 * CH : 3 * CH])
    return sigmoid(gates[:, 3 * CH :]) * jnp.tanh(cell), cell


def updated(cols, blocks, weight, extra, prev):
    rows = prev.shape[0]
    size = rows // blocks
    hs, cs = [], []
    for k in range(blocks):
        part = slice(k * size, (k + 1) * size)
        add = extra if extra.shape[0] == 1 else extra[part]
        h, c = activated(jnp.dot(cols[part, : weight.shape[0]], weight[...], preferred_element_type=F32) + add, prev[part])
        hs.append(h)
        cs.append(c)
    return jnp.concatenate(hs, axis=0), jnp.concatenate(cs, axis=0)


def up_to(v, to):
    return -(-v // to) * to


def geometry(tile, tick, kind):
    n = tile + 6 - 2 * tick
    stride = n + 2
    rows = EDGE if kind else n - 2 * EDGE
    return n, stride, rows, up_to(rows * stride, 16), up_to(rows * n, 8)


def window_taps(src, base, cols_ref, slots, stride, step, first, row):
    for dx in range(3):
        for dy in range(3):
            lane = (3 * dy + dx) * step + first
            start = base + dy * stride + dx
            cols_ref[row : row + slots, lane : lane + CH] = src[start : start + slots, :].astype(BF16)


def sent(tile, tick, kind, h_scr, at, out_scr, send_ref, m_ref):
    n, stride, rows, slots, packed = geometry(tile, tick, kind)
    firsts = (0, n - EDGE) if kind else (EDGE, EDGE)
    for seg, first in enumerate(firsts):
        for r in range(rows):
            src = at + seg * slots + r * stride
            out_scr[seg * packed + r * n : seg * packed + (r + 1) * n, :] = h_scr[src : src + n, :]
        mask = m_ref[first * n : first * n + packed, :]
        send_ref[seg * packed : (seg + 1) * packed, :] = (
            out_scr[seg * packed : (seg + 1) * packed, :] * mask
        ).astype(BF16)


def kept(tile, tick, kind, scr, at, tile_ref):
    _, stride, rows, slots, _ = geometry(tile, tick, kind)
    edge = 3 - tick
    for seg in range(2):
        low, high = (edge, rows) if kind and seg == 0 else (0, rows - edge) if kind else (0, rows)
        for r in range(low, high):
            src = at + seg * slots + r * stride + edge
            v = scr[src : src + tile, :].astype(tile_ref.dtype)
            if kind:
                tile_ref[seg * (rows - edge) + r - low] = v
            else:
                tile_ref[seg, r] = v


def middle_of(batch, k, ref, left_ref, right_ref):
    lanes = slice(k * CH, (k + 1) * CH)
    return middle(ref[batch].astype(F32), left_ref[:, lanes], right_ref[:, lanes], batch)


def first_middle_kernel(blocks, lat_ref, hid_ref, cell_ref, left_ref, right_ref, w_ref, b_ref, m_ref,
                        send_ref, htile_ref, ctile_ref, cols, h_scr, c_scr, out_scr):
    tile = lat_ref.shape[1]
    stride = tile + 8

    @pl.when(lax.axis_index("section") == 0)
    def _():
        rows = (tile + 6 - 2 * EDGE) * stride
        skip = (EDGE - WIDE) * stride
        prev = []
        for batch in range(2):
            for k, ref in enumerate((lat_ref, hid_ref)):
                src = middle_of(batch, k, ref, left_ref, right_ref)[skip:]
                taps(src, WIDE, cols, rows, stride, 2 * CH, k * CH, batch * rows)
            state = rolled(middle_of(batch, 2, cell_ref, left_ref, right_ref), WIDE + 1)
            prev.append(state[skip + stride : skip + stride + rows])
        h, c = updated(cols, blocks, w_ref, b_ref[...], jnp.concatenate(prev))
        h_scr[...] = h
        c_scr[...] = c
        sent(tile, 0, 0, h_scr, 0, out_scr, send_ref, m_ref)
        kept(tile, 0, 0, h_scr, 0, htile_ref)
        kept(tile, 0, 0, c_scr, 0, ctile_ref)


def own_weight(w_ref):
    return jnp.concatenate([w_ref[(2 * t + 1) * CH : (2 * t + 2) * CH, :] for t in range(9)], axis=0)


def bordered(k, ref, batch, left_ref, right_ref, far_ref, near_ref):
    odd = lax.axis_index("row") % 2 == 1
    lanes = slice(k * CH, (k + 1) * CH)
    rows = slice(104 * batch, 104 * (batch + 1))
    far, near = far_ref[rows, lanes].astype(F32), near_ref[rows, lanes].astype(F32)
    above, below = jnp.where(odd, near, far), jnp.where(odd, far, near)
    mid = middle(ref[batch].astype(F32), left_ref[:, lanes], right_ref[:, lanes], batch)
    top = top_half((8, CH))
    first = jnp.where(top, above[96:], mid[:8])
    last = jnp.where(top, mid[384:], below[:8])
    return above[:96], first, mid, last, below[8:]


def first_edge_kernel(blocks, lat_ref, hid_ref, cell_ref, left_ref, right_ref, far_ref, near_ref,
                      w_ref, b_ref, m_ref, _, mid_part_ref, mid_prev_ref, part_ref, prev_ref, *rest):
    sends, tiles, (cols, h_scr, c_scr, out_scr) = rest[:2], rest[2:6], rest[6:]
    tile = lat_ref.shape[1]
    wide = tile + 8
    size = EDGE * wide

    def full(batch, k, ref):
        above, first, mid, last, below = bordered(k, ref, batch, left_ref, right_ref, far_ref, near_ref)
        return jnp.concatenate([above, first, mid[8:384], last, below], axis=0)

    @pl.when(lax.axis_index("section") == 0)
    def _():
        starts = (0, (tile + 6 - EDGE) * wide)
        prev = []
        for batch in range(2):
            for k, ref in enumerate((lat_ref, hid_ref)):
                whole = full(batch, k, ref)
                for half, start in enumerate(starts):
                    src = whole[start : min(start + size + 3 * wide, whole.shape[0])]
                    taps(src, WIDE, cols, size, wide, 2 * CH, k * CH, (2 * batch + half) * size)
            state = rolled(full(batch, 2, cell_ref), WIDE + 1)
            prev += [state[start + wide : start + wide + size] for start in starts]
        h, c = updated(cols.at[: 4 * size], blocks, w_ref, b_ref[...], jnp.concatenate(prev))
        h_scr[: 4 * size, :] = h
        c_scr[: 4 * size, :] = c
        for batch in range(2):
            sent(tile, 0, 1, h_scr, 2 * batch * size, out_scr, sends[batch], m_ref)
            kept(tile, 0, 1, h_scr, 2 * batch * size, tiles[2 * batch])
            kept(tile, 0, 1, c_scr, 2 * batch * size, tiles[2 * batch + 1])

    for s in range(1, LAYERS):

        @pl.when(lax.axis_index("section") == s)
        def _():
            n, stride, _, slots, _ = geometry(tile, s, 1)
            _, _, inner, mid_slots, _ = geometry(tile, s, 0)
            for batch in range(2):
                whole = full(batch, 1, hid_ref)
                h_scr[: whole.shape[0], :] = whole
                c_scr[: whole.shape[0], :] = full(batch, 2, cell_ref)
                segs = (
                    (0, EDGE, slots, 2 * batch * slots, prev_ref, 2 * batch * slots),
                    (n - EDGE, EDGE, slots, (2 * batch + 1) * slots, prev_ref, (2 * batch + 1) * slots),
                    (EDGE, inner, mid_slots, 4 * slots + batch * mid_slots, mid_prev_ref, batch * mid_slots),
                )
                for k, (first, rows, count, row, state_ref, at) in enumerate(segs):
                    base = 320 * k
                    for r in range(rows + 2):
                        src = (s + first + r) * wide + WIDE + s
                        out_scr[base + r * stride : base + (r + 1) * stride, :] = h_scr[src : src + stride, :]
                    window_taps(out_scr, base, cols, count, stride, CH, 0, row)
                    for r in range(rows):
                        src = (s + first + r + 1) * wide + WIDE + 1 + s
                        state_ref[at + r * stride : at + r * stride + n, :] = c_scr[src : src + n, :]
            total = 4 * slots + 2 * mid_slots
            gates = jnp.dot(cols[:total, : 9 * CH], own_weight(w_ref), preferred_element_type=F32) + b_ref[...]
            part_ref[: 4 * slots, :] = gates[: 4 * slots]
            mid_part_ref[: 2 * mid_slots, :] = gates[4 * slots :]


def next_middle_kernel(tick, blocks, x_ref, part_ref, prev_ref, win_ref, m_ref, *rest):
    send_ref, (htile_ref, ctile_ref, cols, h_scr, c_scr, out_scr) = rest[0], rest[-6:]
    tile = htile_ref.shape[2]
    _, stride, _, slots, _ = geometry(tile, tick, 0)
    taken = x_ref.shape[0]

    @pl.when(lax.axis_index("section") == tick)
    def _():
        out_scr[:taken, :] = x_ref[...].astype(F32)
        for batch in range(2):
            window_taps(out_scr, batch * taken // 2, cols, slots, stride, CH, 0, batch * slots)
        h, c = updated(cols, blocks, win_ref, part_ref[: 2 * slots, :], prev_ref[: 2 * slots, :])
        h_scr[...] = h
        c_scr[...] = c
        if tick < LAYERS - 1:
            sent(tile, tick, 0, h_scr, 0, out_scr, send_ref, m_ref)
        kept(tile, tick, 0, h_scr, 0, htile_ref)
        kept(tile, tick, 0, c_scr, 0, ctile_ref)


def next_edge(tick, batch, blocks, tile, x_ref, inner_ref, part_ref, prev_ref, win_ref, cols, h_scr, c_scr, out_scr):
    _, stride, rows, slots, _ = geometry(tile, tick, 1)
    _, _, inner_rows, _, taken = geometry(tile, tick - 1, 0)
    half, two = x_ref.shape[0] // 2, 2 * stride
    x = x_ref[...].astype(F32)
    h_scr[:taken, :] = inner_ref[batch * taken : (batch + 1) * taken, :].astype(F32)
    out_scr[:half, :] = x[:half]
    out_scr[rows * stride : rows * stride + two, :] = h_scr[:two, :]
    out_scr[320 : 320 + two, :] = h_scr[(inner_rows - 2) * stride : inner_rows * stride, :]
    out_scr[320 + two : 320 + two + half, :] = x[half:]
    for seg in range(2):
        window_taps(out_scr, 320 * seg, cols, slots, stride, CH, 0, seg * slots)
    own = slice(2 * slots * batch, 2 * slots * (batch + 1))
    h, c = updated(cols, blocks, win_ref, part_ref[own, :], prev_ref[own, :])
    h_scr[: 2 * slots, :] = h
    c_scr[: 2 * slots, :] = c


def next_edge_kernel(tick, batch, blocks, x_ref, inner_ref, part_ref, prev_ref, win_ref, m_ref,
                     send_ref, htile_ref, ctile_ref, cols, *scr):
    tile = htile_ref.shape[1]

    @pl.when(lax.axis_index("section") == tick)
    def _():
        next_edge(tick, batch, blocks, tile, x_ref, inner_ref, part_ref, prev_ref, win_ref, cols, *scr)
        sent(tile, tick, 1, scr[0], 0, scr[2], send_ref, m_ref)
        kept(tile, tick, 1, scr[0], 0, htile_ref)
        kept(tile, tick, 1, scr[1], 0, ctile_ref)


def stores(tick, batch, tile_ref, out_ref, sems, k):
    tile = out_ref.shape[2]
    part = EDGE - 3 + tick
    if batch is None:
        return [pltpu.make_async_copy(tile_ref, out_ref.at[0, :, pl.ds(part, tile - 2 * part)], sems.at[k])]
    return [
        pltpu.make_async_copy(tile_ref.at[pl.ds(0, part)], out_ref.at[0, batch, pl.ds(0, part)], sems.at[k]),
        pltpu.make_async_copy(
            tile_ref.at[pl.ds(part, part)], out_ref.at[0, batch, pl.ds(tile - part, part)], sems.at[k + 1]
        ),
    ]


def last_kernel(batch, blocks, x_ref, inner_ref, part_ref, prev_ref, win_ref, m_ref, *rest):
    done, (_, _, hout_ref, cout_ref, cols, *scr, htile_ref, ctile_ref, sems) = rest[:-11], rest[-11:]
    tick = LAYERS - 1
    tile = htile_ref.shape[1]

    @pl.when(lax.axis_index("section") == tick)
    def _():
        copies = []
        if batch == 0:
            copies += stores(tick, None, done[0], hout_ref, sems, 4) + stores(tick, None, done[1], cout_ref, sems, 5)
        for copy in copies:
            copy.start()
        next_edge(tick, batch, blocks, tile, x_ref, inner_ref, part_ref, prev_ref, win_ref, cols, *scr)
        kept(tile, tick, 1, scr[1], 0, ctile_ref)
        kept(tile, tick, 1, scr[0], 0, htile_ref)
        mine = stores(tick, batch, ctile_ref, cout_ref, sems, 0) + stores(tick, batch, htile_ref, hout_ref, sems, 2)
        for copy in mine:
            copy.start()
        for copy in copies + mine:
            copy.wait()


def store_kernel(*rest):
    tiles, (hout_ref, cout_ref, sems) = rest[:-3], rest[-3:]
    for tick in range(LAYERS - 1):

        @pl.when(lax.axis_index("section") == tick)
        def _():
            copies = []
            for n, batch in enumerate((None, 0, 1)):
                h, c = tiles[6 * tick + 2 * n : 6 * tick + 2 * n + 2]
                copies += stores(tick, batch, h, hout_ref, sems, 4 * n)
                copies += stores(tick, batch, c, cout_ref, sems, 4 * n + 2)
            for copy in copies:
                copy.start()
            for copy in copies:
                copy.wait()


def on_device(latent, hidden_old, cell_old, weights, bias):
    tile = latent.shape[1]
    n_row, n_col = lax.axis_size("row"), lax.axis_size("col")
    stay = lambda v: pltpu.with_memory_space_constraint(v, pltpu.HBM)
    hid = hidden_old[0]
    cell = cell_old[0]
    w = weights.reshape(-1, weights.shape[-1])

    vm = lambda shape, kind: pltpu.VMEM(shape, kind)
    odd = lambda n: [(i, i + 1) for i in range(1, n - 1, 2)]
    even = lambda n: [(i, i + 1) for i in range(0, n - 1, 2)]
    both = lambda pairs: pairs + [(j, i) for i, j in pairs]
    lat, hid, cell, left, right = call(
        pack_kernel,
        (stay(latent), stay(hid), stay(cell)),
        [ANY] * 3,
        [vm(latent.shape, BF16), vm(hid.shape, BF16), vm(cell.shape, F32)] + [vm((8 * tile, 3 * CH), BF16)] * 2,
        [VMEM] * 5,
        [pltpu.SemaphoreType.DMA((3,))],
    )
    w, b, win, mask = call(
        functools.partial(load_kernel, tile),
        (right, stay(w), stay(bias)),
        [VMEM, ANY, ANY],
        [vm(w.shape, BF16), vm(bias.shape, F32), vm((9 * CH, 4 * CH), BF16), vm((up_to((tile + 6) ** 2, 8) + 16, CH), F32)],
        [VMEM] * 4,
        [pltpu.SemaphoreType.DMA((2,))],
        flops=1 << 31,
    )
    left = lax.ppermute(left, "col", both(odd(n_col)))
    right = lax.ppermute(right, "col", both(even(n_col)))

    far, near = call(
        middle_kernel, (lat, hid, cell, left, right, b), [VMEM] * 6, [vm((208, 3 * CH), BF16)] * 2, [VMEM] * 2
    )
    far = lax.ppermute(far, "row", both(odd(n_row)))
    near = lax.ppermute(near, "row", both(even(n_row)))

    def scratch(slots, lanes, work=0):
        sizes = (work or slots, work or slots, max(960, slots))
        return [pltpu.VMEM((slots, lanes), BF16)] + [pltpu.VMEM((size, CH), F32) for size in sizes]

    def sizes(tick, kind):
        return tuple(2 * v for v in geometry(tile, tick, kind)[3:])

    def tiles_of(tick, kind):
        part = EDGE - 3 + tick
        shape = (2 * part, tile, CH) if kind else (2, tile - 2 * part, tile, CH)
        return [vm(shape, BF16), vm(shape, F32)]

    def hop(v, tick):
        return lax.ppermute(v, "section", [(tick, tick + 1)])

    slots, packed = sizes(0, 0)
    send, htile, ctile = call(
        functools.partial(first_middle_kernel, BLOCKS),
        (lat, hid, cell, left, right, w, b, mask),
        [VMEM] * 8,
        [vm((packed, CH), BF16)] + tiles_of(0, 0),
        [VMEM] * 3,
        scratch(slots, 18 * CH),
        flops=2 * slots * 2304 * 512,
    )
    xs, tiles = [hop(send, 0)], [htile, ctile]
    slots, packed = sizes(0, 1)
    inner, outer = sizes(1, 0)[0], 2 * sizes(1, 1)[0]
    *state, first, second, h0, c0, h1, c1 = call(
        functools.partial(first_edge_kernel, BLOCKS),
        (lat, hid, cell, left, right, far, near, w, b, mask, htile),
        [VMEM] * 11,
        [vm((rows, width), F32) for rows in (inner, outer) for width in (4 * CH, CH)]
        + [vm((packed, CH), BF16)] * 2
        + tiles_of(0, 1) * 2,
        [VMEM] * 10,
        scratch(max(2 * slots, outer + inner), 18 * CH, 640),
        flops=4 * slots * 2304 * 512,
    )
    state = (state[:2], state[2:])
    xs += [hop(first, 0), hop(second, 0)]
    tiles += [h0, c0, h1, c1]

    out_shapes = [
        jax.ShapeDtypeStruct((1, 2, tile, tile, CH), BF16),
        jax.ShapeDtypeStruct((1, 2, tile, tile, CH), F32),
    ]
    for tick in range(1, LAYERS):
        last = tick == LAYERS - 1
        slots, packed = sizes(tick, 0)
        result = call(
            functools.partial(next_middle_kernel, tick, BLOCKS),
            (xs[0], *state[0], win, mask),
            [VMEM] * 5,
            ([] if last else [vm((packed, CH), BF16)]) + tiles_of(tick, 0),
            [VMEM] * (2 if last else 3),
            scratch(slots, 9 * CH),
            flops=2 * slots * 1152 * 512,
        )
        slots, packed = sizes(tick, 1)
        mine = list(result[-2:])
        nxt = [] if last else [hop(result[0], tick)]
        for batch in range(2):
            ins = (xs[1 + batch], xs[0], *state[1], win, mask)
            scr = scratch(slots, 9 * CH, 320)
            if last:
                done = tuple(mine) if batch == 0 else ()
                count = len(ins) + len(done)
                outs = call(
                    functools.partial(last_kernel, batch, BLOCKS),
                    (*ins, *done, *outs),
                    [VMEM] * count + [ANY] * 2,
                    out_shapes,
                    [ANY, ANY],
                    scr + tiles_of(tick, 1) + [pltpu.SemaphoreType.DMA((6,))],
                    aliases={count: 0, count + 1: 1},
                    flops=2 * slots * 1152 * 512,
                )
                continue
            send, *result = call(
                functools.partial(next_edge_kernel, tick, batch, BLOCKS),
                ins,
                [VMEM] * len(ins),
                [vm((packed, CH), BF16)] + tiles_of(tick, 1),
                [VMEM] * 3,
                scr,
                flops=2 * slots * 1152 * 512,
                after=mine[-2],
            )
            mine += result
            nxt.append(hop(send, tick))
        xs = nxt
        tiles += mine
        if tick == LAYERS - 2:
            outs = call(
                store_kernel, (*tiles,), [VMEM] * len(tiles), out_shapes, [ANY, ANY], [pltpu.SemaphoreType.DMA((12,))]
            )
    return tuple(outs)


def solution(mesh):
    in_specs = (
        P(None, "row", "col", None),
        P("section", None, "row", "col", None),
        P("section", None, "row", "col", None),
        P("section", None, None, None),
        P("section", None),
    )
    out_specs = (P("section", None, "row", "col", None), P("section", None, "row", "col", None))

    return jax.shard_map(on_device, mesh=mesh, in_specs=in_specs, out_specs=out_specs, check_vma=False)
```

```python
import functools

import jax
import jax.numpy as jnp
from jax import lax
from jax.experimental import pallas as pl
from jax.experimental.pallas import tpu as pltpu
from jax.sharding import PartitionSpec as P


F32 = jnp.float32
BF16 = jnp.bfloat16
CH = 128
LAYERS = 4
BLOCKS = 1
EDGE = 6
WIDE = 4
VMEM = pl.BlockSpec(memory_space=pltpu.VMEM)
ANY = pl.BlockSpec(memory_space=pl.ANY)


def sigmoid(x):
    return 0.5 * jnp.tanh(0.5 * x) + 0.5


def rolled(x, by):
    rows = x.shape[0]
    by = by % rows
    return x if by == 0 else pltpu.roll(x, rows - by, 0)


def swap_halves(x):
    tiles = x.shape[0]
    flat = x.reshape(tiles * 8, CH)
    up, down = pltpu.roll(flat, 4, 0), pltpu.roll(flat, tiles * 8 - 4, 0)
    return jnp.where(top_half(flat.shape), down, up).reshape(x.shape)


def top_half(shape):
    return lax.broadcasted_iota(jnp.int32, shape, len(shape) - 2) % 8 < 4


def call(kernel, ins, in_specs, outs, out_specs, scratch=(), aliases=None, flops=0, limit=16, after=None):
    body = kernel
    if after is not None:
        ins, in_specs = (*ins, after), [*in_specs, VMEM]
        body = lambda *refs: kernel(*refs[: len(ins) - 1], *refs[len(ins) :])
    return pl.pallas_call(
        body,
        out_shape=tuple(outs),
        in_specs=in_specs,
        out_specs=tuple(out_specs),
        scratch_shapes=list(scratch),
        input_output_aliases=aliases or {},
        compiler_params=pltpu.CompilerParams(vmem_limit_bytes=limit << 20),
        cost_estimate=pl.CostEstimate(flops=flops, bytes_accessed=1 << 20, transcendentals=0),
    )(*ins)


def pack_kernel(lat_hbm, hid_hbm, cell_hbm, lat_ref, hid_ref, cell_ref, far_ref, near_ref, sems):
    odd = lax.axis_index("col") % 2 == 1
    copies = [
        pltpu.make_async_copy(src, dst, sems.at[k])
        for k, (src, dst) in enumerate(((lat_hbm, lat_ref), (hid_hbm, hid_ref), (cell_hbm, cell_ref)))
    ]
    for copy in copies:
        copy.start()
    for k, ref in enumerate((lat_ref, hid_ref, cell_ref)):
        copies[k].wait()
        first, second = ref[0].astype(F32), ref[1].astype(F32)
        tile = first.shape[0]
        top = top_half((tile, 8, CH))
        lanes = slice(k * CH, (k + 1) * CH)
        low = jnp.where(top, first[:, :8], swap_halves(second[:, :8]))
        high = jnp.where(top, swap_halves(first[:, 8:]), second[:, 8:])
        low, high = (v.reshape(tile * 8, CH).astype(BF16) for v in (low, high))

        @pl.when(odd)
        def _():
            far_ref[:, lanes] = high
            near_ref[:, lanes] = low

        @pl.when(jnp.logical_not(odd))
        def _():
            far_ref[:, lanes] = low
            near_ref[:, lanes] = high


def load_kernel(tile, _, w_hbm, b_hbm, w_ref, b_ref, win_ref, m_ref, sems):
    copies = [pltpu.make_async_copy(w_hbm, w_ref, sems.at[0]), pltpu.make_async_copy(b_hbm, b_ref, sems.at[1])]
    for copy in copies:
        copy.start()
    high, width = lax.axis_size("row") * tile, lax.axis_size("col") * tile
    for s in range(LAYERS - 1):

        @pl.when(lax.axis_index("section") == s)
        def _():
            n = tile + 6 - 2 * s
            shape = (n, tile + 8, CH)
            r = lax.axis_index("row") * tile - (3 - s) + lax.broadcasted_iota(jnp.int32, shape, 0)
            c = lax.axis_index("col") * tile - (3 - s) + lax.broadcasted_iota(jnp.int32, shape, 1)
            inside = (r >= 0) & (r < high) & (c >= 0) & (c < width)
            wide = jnp.where(inside, jnp.ones(shape, F32), jnp.zeros(shape, F32))
            m_ref[n * n :, :] = jnp.zeros((m_ref.shape[0] - n * n, CH), F32)
            for k in range(n):
                m_ref[k * n : (k + 1) * n, :] = wide[k][:n]

    for copy in copies:
        copy.wait()

    @pl.when(lax.axis_index("section") > 0)
    def _():
        for t in range(9):
            win_ref[t * CH : (t + 1) * CH, :] = w_ref[2 * t * CH : (2 * t + 1) * CH, :]


def middle(own, far, near, batch):
    tile = own.shape[0]
    far, near = (v.astype(F32).reshape(tile, 8, CH) for v in (far, near))
    odd = lax.axis_index("col") % 2 == 1
    left, right = jnp.where(odd, near, far), jnp.where(odd, far, near)
    if batch == 0:
        left = swap_halves(left)
    else:
        right = swap_halves(right)
    top = top_half((tile, 8, CH))
    zero = jnp.zeros((1, 8, CH), F32)
    side = jnp.where(top, right, jnp.concatenate([left[1:], zero], axis=0))
    rows = jnp.concatenate([own, side], axis=1).reshape(tile * (tile + 8), CH)
    return jnp.concatenate([left[0], rows], axis=0)


def middle_kernel(lat_ref, hid_ref, cell_ref, left_ref, right_ref, _, far_ref, near_ref):
    odd = lax.axis_index("row") % 2 == 1
    for batch in range(2):
        for k, ref in enumerate((lat_ref, hid_ref, cell_ref)):
            lanes = slice(k * CH, (k + 1) * CH)
            mid = middle(ref[batch].astype(F32), left_ref[:, lanes], right_ref[:, lanes], batch)
            up, down = mid[:104].astype(BF16), mid[288:].astype(BF16)
            rows = slice(104 * batch, 104 * (batch + 1))

            @pl.when(odd)
            def _():
                far_ref[rows, lanes] = down
                near_ref[rows, lanes] = up

            @pl.when(jnp.logical_not(odd))
            def _():
                far_ref[rows, lanes] = up
                near_ref[rows, lanes] = down


def taps(src, at, cols_ref, rows, stride, step, first, row=0):
    for dx in range(3):
        moved = rolled(src, at + dx)
        for dy in range(3):
            lane = (3 * dy + dx) * step + first
            start = dy * stride
            cols_ref[row : row + rows, lane : lane + CH] = moved[start : start + rows].astype(BF16)


def activated(gates, cell_prev):
    cell = sigmoid(gates[:, CH : 2 * CH]) * cell_prev + sigmoid(gates[:, :CH]) * jnp.tanh(gates[:, 2 * CH : 3 * CH])
    return sigmoid(gates[:, 3 * CH :]) * jnp.tanh(cell), cell


def updated(cols, blocks, weight, extra, prev):
    rows = prev.shape[0]
    size = rows // blocks
    hs, cs = [], []
    for k in range(blocks):
        part = slice(k * size, (k + 1) * size)
        add = extra if extra.shape[0] == 1 else extra[part]
        h, c = activated(jnp.dot(cols[part, : weight.shape[0]], weight[...], preferred_element_type=F32) + add, prev[part])
        hs.append(h)
        cs.append(c)
    return jnp.concatenate(hs, axis=0), jnp.concatenate(cs, axis=0)


def up_to(v, to):
    return -(-v // to) * to


def geometry(tile, tick, kind):
    n = tile + 6 - 2 * tick
    stride = n + 2
    rows = EDGE if kind else n - 2 * EDGE
    return n, stride, rows, up_to(rows * stride, 16), up_to(rows * n, 8)


def window_taps(src, base, cols_ref, slots, stride, step, first, row):
    for dx in range(3):
        for dy in range(3):
            lane = (3 * dy + dx) * step + first
            start = base + dy * stride + dx
            cols_ref[row : row + slots, lane : lane + CH] = src[start : start + slots, :].astype(BF16)


def sent(tile, tick, kind, h_scr, at, out_scr, send_ref, m_ref):
    n, stride, rows, slots, packed = geometry(tile, tick, kind)
    firsts = (0, n - EDGE) if kind else (EDGE, EDGE)
    for seg, first in enumerate(firsts):
        for r in range(rows):
            src = at + seg * slots + r * stride
            out_scr[seg * packed + r * n : seg * packed + (r + 1) * n, :] = h_scr[src : src + n, :]
        mask = m_ref[first * n : first * n + packed, :]
        send_ref[seg * packed : (seg + 1) * packed, :] = (
            out_scr[seg * packed : (seg + 1) * packed, :] * mask
        ).astype(BF16)


def kept(tile, tick, kind, scr, at, tile_ref):
    _, stride, rows, slots, _ = geometry(tile, tick, kind)
    edge = 3 - tick
    for seg in range(2):
        low, high = (edge, rows) if kind and seg == 0 else (0, rows - edge) if kind else (0, rows)
        for r in range(low, high):
            src = at + seg * slots + r * stride + edge
            v = scr[src : src + tile, :].astype(tile_ref.dtype)
            if kind:
                tile_ref[seg * (rows - edge) + r - low] = v
            else:
                tile_ref[seg, r] = v


def middle_of(batch, k, ref, left_ref, right_ref):
    lanes = slice(k * CH, (k + 1) * CH)
    return middle(ref[batch].astype(F32), left_ref[:, lanes], right_ref[:, lanes], batch)


def first_middle_kernel(blocks, lat_ref, hid_ref, cell_ref, left_ref, right_ref, w_ref, b_ref, m_ref,
                        send_ref, htile_ref, ctile_ref, cols, h_scr, c_scr, out_scr):
    tile = lat_ref.shape[1]
    stride = tile + 8

    @pl.when(lax.axis_index("section") == 0)
    def _():
        rows = (tile + 6 - 2 * EDGE) * stride
        skip = (EDGE - WIDE) * stride
        prev = []
        for batch in range(2):
            for k, ref in enumerate((lat_ref, hid_ref)):
                src = middle_of(batch, k, ref, left_ref, right_ref)[skip:]
                taps(src, WIDE, cols, rows, stride, 2 * CH, k * CH, batch * rows)
            state = rolled(middle_of(batch, 2, cell_ref, left_ref, right_ref), WIDE + 1)
            prev.append(state[skip + stride : skip + stride + rows])
        h, c = updated(cols, blocks, w_ref, b_ref[...], jnp.concatenate(prev))
        h_scr[...] = h
        c_scr[...] = c
        sent(tile, 0, 0, h_scr, 0, out_scr, send_ref, m_ref)
        kept(tile, 0, 0, h_scr, 0, htile_ref)
        kept(tile, 0, 0, c_scr, 0, ctile_ref)


def own_weight(w_ref):
    return jnp.concatenate([w_ref[(2 * t + 1) * CH : (2 * t + 2) * CH, :] for t in range(9)], axis=0)


def bordered(k, ref, batch, left_ref, right_ref, far_ref, near_ref):
    odd = lax.axis_index("row") % 2 == 1
    lanes = slice(k * CH, (k + 1) * CH)
    rows = slice(104 * batch, 104 * (batch + 1))
    far, near = far_ref[rows, lanes].astype(F32), near_ref[rows, lanes].astype(F32)
    above, below = jnp.where(odd, near, far), jnp.where(odd, far, near)
    mid = middle(ref[batch].astype(F32), left_ref[:, lanes], right_ref[:, lanes], batch)
    top = top_half((8, CH))
    first = jnp.where(top, above[96:], mid[:8])
    last = jnp.where(top, mid[384:], below[:8])
    return above[:96], first, mid, last, below[8:]


def first_edge_kernel(batch, blocks, lat_ref, hid_ref, cell_ref, left_ref, right_ref, far_ref, near_ref,
                      w_ref, b_ref, m_ref, _, *rest):
    send_ref, htile_ref, ctile_ref, cols, h_scr, c_scr, out_scr = rest[-7:]
    tile = lat_ref.shape[1]
    wide = tile + 8
    size = EDGE * wide

    def full(batch, k, ref):
        above, first, mid, last, below = bordered(k, ref, batch, left_ref, right_ref, far_ref, near_ref)
        return jnp.concatenate([above, first, mid[8:384], last, below], axis=0)

    @pl.when(lax.axis_index("section") == 0)
    def _():
        starts = (0, (tile + 6 - EDGE) * wide)
        for k, ref in enumerate((lat_ref, hid_ref)):
            whole = full(batch, k, ref)
            for half, start in enumerate(starts):
                src = whole[start : min(start + size + 3 * wide, whole.shape[0])]
                taps(src, WIDE, cols, size, wide, 2 * CH, k * CH, half * size)
        state = rolled(full(batch, 2, cell_ref), WIDE + 1)
        prev = [state[start + wide : start + wide + size] for start in starts]
        h, c = updated(cols.at[: 2 * size], blocks, w_ref, b_ref[...], jnp.concatenate(prev))
        h_scr[: 2 * size, :] = h
        c_scr[: 2 * size, :] = c
        sent(tile, 0, 1, h_scr, 0, out_scr, send_ref, m_ref)
        kept(tile, 0, 1, h_scr, 0, htile_ref)
        kept(tile, 0, 1, c_scr, 0, ctile_ref)

    if batch == 0:
        return
    mid_part_ref, mid_prev_ref, part_ref, prev_ref = rest[:4]
    for s in range(1, LAYERS):

        @pl.when(lax.axis_index("section") == s)
        def _():
            n, stride, _, slots, _ = geometry(tile, s, 1)
            _, _, inner, mid_slots, _ = geometry(tile, s, 0)
            for batch in range(2):
                whole = full(batch, 1, hid_ref)
                h_scr[: whole.shape[0], :] = whole
                c_scr[: whole.shape[0], :] = full(batch, 2, cell_ref)
                segs = (
                    (0, EDGE, slots, 2 * batch * slots, prev_ref, 2 * batch * slots),
                    (n - EDGE, EDGE, slots, (2 * batch + 1) * slots, prev_ref, (2 * batch + 1) * slots),
                    (EDGE, inner, mid_slots, 4 * slots + batch * mid_slots, mid_prev_ref, batch * mid_slots),
                )
                for k, (first, rows, count, row, state_ref, at) in enumerate(segs):
                    base = 320 * k
                    for r in range(rows + 2):
                        src = (s + first + r) * wide + WIDE + s
                        out_scr[base + r * stride : base + (r + 1) * stride, :] = h_scr[src : src + stride, :]
                    window_taps(out_scr, base, cols, count, stride, CH, 0, row)
                    for r in range(rows):
                        src = (s + first + r + 1) * wide + WIDE + 1 + s
                        state_ref[at + r * stride : at + r * stride + n, :] = c_scr[src : src + n, :]
            total = 4 * slots + 2 * mid_slots
            gates = jnp.dot(cols[:total, : 9 * CH], own_weight(w_ref), preferred_element_type=F32) + b_ref[...]
            part_ref[: 4 * slots, :] = gates[: 4 * slots]
            mid_part_ref[: 2 * mid_slots, :] = gates[4 * slots :]


def next_middle_kernel(tick, blocks, x_ref, part_ref, prev_ref, win_ref, m_ref, *rest):
    send_ref, (htile_ref, ctile_ref, cols, h_scr, c_scr, out_scr) = rest[0], rest[-6:]
    tile = htile_ref.shape[2]
    _, stride, _, slots, _ = geometry(tile, tick, 0)
    taken = x_ref.shape[0]

    @pl.when(lax.axis_index("section") == tick)
    def _():
        out_scr[:taken, :] = x_ref[...].astype(F32)
        for batch in range(2):
            window_taps(out_scr, batch * taken // 2, cols, slots, stride, CH, 0, batch * slots)
        h, c = updated(cols, blocks, win_ref, part_ref[: 2 * slots, :], prev_ref[: 2 * slots, :])
        h_scr[...] = h
        c_scr[...] = c
        if tick < LAYERS - 1:
            sent(tile, tick, 0, h_scr, 0, out_scr, send_ref, m_ref)
        kept(tile, tick, 0, h_scr, 0, htile_ref)
        kept(tile, tick, 0, c_scr, 0, ctile_ref)


def next_edge(tick, batch, blocks, tile, x_ref, inner_ref, part_ref, prev_ref, win_ref, cols, h_scr, c_scr, out_scr):
    _, stride, rows, slots, _ = geometry(tile, tick, 1)
    _, _, inner_rows, _, taken = geometry(tile, tick - 1, 0)
    half, two = x_ref.shape[0] // 2, 2 * stride
    x = x_ref[...].astype(F32)
    h_scr[:taken, :] = inner_ref[batch * taken : (batch + 1) * taken, :].astype(F32)
    out_scr[:half, :] = x[:half]
    out_scr[rows * stride : rows * stride + two, :] = h_scr[:two, :]
    out_scr[320 : 320 + two, :] = h_scr[(inner_rows - 2) * stride : inner_rows * stride, :]
    out_scr[320 + two : 320 + two + half, :] = x[half:]
    for seg in range(2):
        window_taps(out_scr, 320 * seg, cols, slots, stride, CH, 0, seg * slots)
    own = slice(2 * slots * batch, 2 * slots * (batch + 1))
    h, c = updated(cols, blocks, win_ref, part_ref[own, :], prev_ref[own, :])
    h_scr[: 2 * slots, :] = h
    c_scr[: 2 * slots, :] = c


def next_edge_kernel(tick, batch, blocks, x_ref, inner_ref, part_ref, prev_ref, win_ref, m_ref,
                     send_ref, htile_ref, ctile_ref, cols, *scr):
    tile = htile_ref.shape[1]

    @pl.when(lax.axis_index("section") == tick)
    def _():
        next_edge(tick, batch, blocks, tile, x_ref, inner_ref, part_ref, prev_ref, win_ref, cols, *scr)
        sent(tile, tick, 1, scr[0], 0, scr[2], send_ref, m_ref)
        kept(tile, tick, 1, scr[0], 0, htile_ref)
        kept(tile, tick, 1, scr[1], 0, ctile_ref)


def stores(tick, batch, tile_ref, out_ref, sems, k):
    tile = out_ref.shape[2]
    part = EDGE - 3 + tick
    if batch is None:
        return [pltpu.make_async_copy(tile_ref, out_ref.at[0, :, pl.ds(part, tile - 2 * part)], sems.at[k])]
    return [
        pltpu.make_async_copy(tile_ref.at[pl.ds(0, part)], out_ref.at[0, batch, pl.ds(0, part)], sems.at[k]),
        pltpu.make_async_copy(
            tile_ref.at[pl.ds(part, part)], out_ref.at[0, batch, pl.ds(tile - part, part)], sems.at[k + 1]
        ),
    ]


def last_kernel(batch, blocks, x_ref, inner_ref, part_ref, prev_ref, win_ref, m_ref, *rest):
    done, (_, _, hout_ref, cout_ref, cols, *scr, htile_ref, ctile_ref, sems) = rest[:-11], rest[-11:]
    tick = LAYERS - 1
    tile = htile_ref.shape[1]

    @pl.when(lax.axis_index("section") == tick)
    def _():
        copies = []
        if batch == 0:
            copies += stores(tick, None, done[0], hout_ref, sems, 4) + stores(tick, None, done[1], cout_ref, sems, 5)
        for copy in copies:
            copy.start()
        next_edge(tick, batch, blocks, tile, x_ref, inner_ref, part_ref, prev_ref, win_ref, cols, *scr)
        kept(tile, tick, 1, scr[1], 0, ctile_ref)
        kept(tile, tick, 1, scr[0], 0, htile_ref)
        mine = stores(tick, batch, ctile_ref, cout_ref, sems, 0) + stores(tick, batch, htile_ref, hout_ref, sems, 2)
        for copy in mine:
            copy.start()
        for copy in copies + mine:
            copy.wait()


def store_kernel(*rest):
    tiles, (hout_ref, cout_ref, sems) = rest[:-3], rest[-3:]
    for tick in range(LAYERS - 1):

        @pl.when(lax.axis_index("section") == tick)
        def _():
            copies = []
            for n, batch in enumerate((None, 0, 1)):
                h, c = tiles[6 * tick + 2 * n : 6 * tick + 2 * n + 2]
                copies += stores(tick, batch, h, hout_ref, sems, 4 * n)
                copies += stores(tick, batch, c, cout_ref, sems, 4 * n + 2)
            for copy in copies:
                copy.start()
            for copy in copies:
                copy.wait()


def on_device(latent, hidden_old, cell_old, weights, bias):
    tile = latent.shape[1]
    n_row, n_col = lax.axis_size("row"), lax.axis_size("col")
    stay = lambda v: pltpu.with_memory_space_constraint(v, pltpu.HBM)
    hid = hidden_old[0]
    cell = cell_old[0]
    w = weights.reshape(-1, weights.shape[-1])

    vm = lambda shape, kind: pltpu.VMEM(shape, kind)
    odd = lambda n: [(i, i + 1) for i in range(1, n - 1, 2)]
    even = lambda n: [(i, i + 1) for i in range(0, n - 1, 2)]
    both = lambda pairs: pairs + [(j, i) for i, j in pairs]
    lat, hid, cell, left, right = call(
        pack_kernel,
        (stay(latent), stay(hid), stay(cell)),
        [ANY] * 3,
        [vm(latent.shape, BF16), vm(hid.shape, BF16), vm(cell.shape, F32)] + [vm((8 * tile, 3 * CH), BF16)] * 2,
        [VMEM] * 5,
        [pltpu.SemaphoreType.DMA((3,))],
    )
    w, b, win, mask = call(
        functools.partial(load_kernel, tile),
        (right, stay(w), stay(bias)),
        [VMEM, ANY, ANY],
        [vm(w.shape, BF16), vm(bias.shape, F32), vm((9 * CH, 4 * CH), BF16), vm((up_to((tile + 6) ** 2, 8) + 16, CH), F32)],
        [VMEM] * 4,
        [pltpu.SemaphoreType.DMA((2,))],
        flops=1 << 31,
    )
    left = lax.ppermute(left, "col", both(odd(n_col)))
    right = lax.ppermute(right, "col", both(even(n_col)))

    far, near = call(
        middle_kernel, (lat, hid, cell, left, right, b), [VMEM] * 6, [vm((208, 3 * CH), BF16)] * 2, [VMEM] * 2
    )
    far = lax.ppermute(far, "row", both(odd(n_row)))
    near = lax.ppermute(near, "row", both(even(n_row)))

    def scratch(slots, lanes, work=0):
        sizes = (work or slots, work or slots, max(960, slots))
        return [pltpu.VMEM((slots, lanes), BF16)] + [pltpu.VMEM((size, CH), F32) for size in sizes]

    def sizes(tick, kind):
        return tuple(2 * v for v in geometry(tile, tick, kind)[3:])

    def tiles_of(tick, kind):
        part = EDGE - 3 + tick
        shape = (2 * part, tile, CH) if kind else (2, tile - 2 * part, tile, CH)
        return [vm(shape, BF16), vm(shape, F32)]

    def hop(v, tick):
        return lax.ppermute(v, "section", [(tick, tick + 1)])

    slots, packed = sizes(0, 0)
    send, htile, ctile = call(
        functools.partial(first_middle_kernel, BLOCKS),
        (lat, hid, cell, left, right, w, b, mask),
        [VMEM] * 8,
        [vm((packed, CH), BF16)] + tiles_of(0, 0),
        [VMEM] * 3,
        scratch(slots, 18 * CH),
        flops=2 * slots * 2304 * 512,
    )
    xs, tiles = [hop(send, 0)], [htile, ctile]
    slots, packed = sizes(0, 1)
    inner, outer = sizes(1, 0)[0], 2 * sizes(1, 1)[0]
    for batch in range(2):
        extra = [vm((rows, width), F32) for rows in (inner, outer) for width in (4 * CH, CH)] if batch else []
        *state, send, htile, ctile = call(
            functools.partial(first_edge_kernel, batch, BLOCKS),
            (lat, hid, cell, left, right, far, near, w, b, mask, htile),
            [VMEM] * 11,
            extra + [vm((packed, CH), BF16)] + tiles_of(0, 1),
            [VMEM] * (3 + len(extra)),
            scratch(max(slots, outer + inner), 18 * CH, 640),
            flops=2 * slots * 2304 * 512,
        )
        xs.append(hop(send, 0))
        tiles += [htile, ctile]
    state = (state[:2], state[2:])

    out_shapes = [
        jax.ShapeDtypeStruct((1, 2, tile, tile, CH), BF16),
        jax.ShapeDtypeStruct((1, 2, tile, tile, CH), F32),
    ]
    for tick in range(1, LAYERS):
        last = tick == LAYERS - 1
        slots, packed = sizes(tick, 0)
        result = call(
            functools.partial(next_middle_kernel, tick, BLOCKS),
            (xs[0], *state[0], win, mask),
            [VMEM] * 5,
            ([] if last else [vm((packed, CH), BF16)]) + tiles_of(tick, 0),
            [VMEM] * (2 if last else 3),
            scratch(slots, 9 * CH),
            flops=2 * slots * 1152 * 512,
        )
        slots, packed = sizes(tick, 1)
        mine = list(result[-2:])
        nxt = [] if last else [hop(result[0], tick)]
        for batch in range(2):
            ins = (xs[1 + batch], xs[0], *state[1], win, mask)
            scr = scratch(slots, 9 * CH, 320)
            if last:
                done = tuple(mine) if batch == 0 else ()
                count = len(ins) + len(done)
                outs = call(
                    functools.partial(last_kernel, batch, BLOCKS),
                    (*ins, *done, *outs),
                    [VMEM] * count + [ANY] * 2,
                    out_shapes,
                    [ANY, ANY],
                    scr + tiles_of(tick, 1) + [pltpu.SemaphoreType.DMA((6,))],
                    aliases={count: 0, count + 1: 1},
                    flops=2 * slots * 1152 * 512,
                )
                continue
            send, *result = call(
                functools.partial(next_edge_kernel, tick, batch, BLOCKS),
                ins,
                [VMEM] * len(ins),
                [vm((packed, CH), BF16)] + tiles_of(tick, 1),
                [VMEM] * 3,
                scr,
                flops=2 * slots * 1152 * 512,
                after=mine[-2],
            )
            mine += result
            nxt.append(hop(send, tick))
        xs = nxt
        tiles += mine
        if tick == LAYERS - 2:
            outs = call(
                store_kernel, (*tiles,), [VMEM] * len(tiles), out_shapes, [ANY, ANY], [pltpu.SemaphoreType.DMA((12,))]
            )
    return tuple(outs)


def solution(mesh):
    in_specs = (
        P(None, "row", "col", None),
        P("section", None, "row", "col", None),
        P("section", None, "row", "col", None),
        P("section", None, None, None),
        P("section", None),
    )
    out_specs = (P("section", None, "row", "col", None), P("section", None, "row", "col", None))

    return jax.shard_map(on_device, mesh=mesh, in_specs=in_specs, out_specs=out_specs, check_vma=False)
```
